32 devices in a mesh: dp: 4 (over y, x), ctx: 4 (over z), tp: 2 (over core).
Axes of the slice: x: 2, y: 2, z: 4, core: 2. Of those that a mesh axis runs over, the one named last changes fastest.
Arguments:
- tokens: bfloat16 [8, 2048, 768], P('dp', 'ctx'), may hold values from -6 to 6
- segments: int32 [8, 2048], P('dp', 'ctx'), may hold values from 0 to 7, never falling along the last dimension, each value on 1 to 768 neighbouring positions
- cotangent: bfloat16 [8, 2048, 768], P('dp', 'ctx'), may hold values from -6 to 6
- w_qkv: bfloat16 [768, 3, 768], P('dp', None, 'tp'), may hold values from -0.21875 to 0.21875
- w_out: bfloat16 [768, 768], P('dp', 'tp'), may hold values from -1.75 to 1.75
- w_gate: bfloat16 [768, 3072], P('dp', 'tp'), may hold values from -0.21875 to 0.21875
- w_up: bfloat16 [768, 3072], P('dp', 'tp'), may hold values from -0.21875 to 0.21875
- w_down: bfloat16 [768, 3072], P('dp', 'tp'), may hold values from -0.109375 to 0.109375
- norm_gain: bfloat16 [768], P('dp'), may hold values from 0.5 to 1.5
- norm_bias: bfloat16 [768], P('dp'), may hold values from -3 to 3
- final_gain: bfloat16 [768], P('dp'), may hold values from 0.5 to 1.5
- final_bias: bfloat16 [768], P('dp'), may hold values from -3 to 3
Outputs:
- output: bfloat16 [8, 2048, 768], P('dp', 'ctx')
- d_tokens: bfloat16 [8, 2048, 768], P('dp', 'ctx')
- d_qkv: float32 [768, 3, 768], P('dp', None, 'tp')
- d_out: float32 [768, 768], P('dp', 'tp')
- d_gate: float32 [768, 3072], P('dp', 'tp')
- d_up: float32 [768, 3072], P('dp', 'tp')
- d_down: float32 [768, 3072], P('dp', 'tp')
- d_norm_gain: float32 [768], P('dp')
- d_norm_bias: float32 [768], P('dp')
- d_final_gain: float32 [768], P('dp')
- d_final_bias: float32 [768], P('dp')
The draws below stay inside these ranges and needn't reach their ends.
Inputs may be any that keep to these rules, and one draw needn't show every extreme that they name: `segments`: within each sequence the segment numbers never fall, and each document is a run of consecutive tokens.
All inputs are finite; a program needn't handle non-finite values.
Results may differ from the reference program's by a relative error of at most 0.023.
Values may be sent and summed in bfloat16 or wider, within the bound.
No kernel may reach another device: no remote copies, remote signals or barrier semaphores. Data moves between devices by JAX's collectives and lax.ppermute only.
A program may use at most 192 MiB of HBM per device.

```python
import math
import jax
import jax.numpy as jnp
import numpy as np
from jax import lax

D = 768
H = 12
HD = 64
FF = 3072
LEN = 2048
NSEQ = 8


def block_scale(key, extent, split, least, largest):
    def one(position, parts):
        heights = jax.random.uniform(jax.random.fold_in(jax.random.fold_in(key, 6), position), (parts,), jnp.float32, least / len(split), largest / len(split))
        return jnp.repeat(jnp.exp(heights), extent[position] // parts).reshape((-1,) + (1,) * (len(extent) - position - 1))

    loudness = one(*split[0])
    for cut in split[1:]:
        loudness = loudness * one(*cut)
    return loudness


def length_profile(number_of, total, bound, skew):
    weights = [(1 << 20) // math.isqrt(grade ** skew) + 1 for grade in range(2, number_of + 1)]
    spare, given = total - bound - (number_of - 1), [1] * (number_of - 1)
    while spare > 0:
        free = [i for i in range(number_of - 1) if given[i] < bound]
        whole, budget = sum([weights[i] for i in free]), spare
        for i in free:
            more = min(bound - given[i], max(1, budget * weights[i] // whole), spare)
            given[i] = given[i] + more
            spare = spare - more
    return np.array([bound] + given)


def ragged_sizes(stream_key, number_of, total, limit, slope):
    if number_of == 2:
        one = jax.random.randint(stream_key, (), max(1, total - limit), min(limit, total - 1) + 1)
        return jnp.stack([one, total - one])
    lengths = jnp.asarray(length_profile(number_of, total, limit, slope), jnp.int32)
    pairs = (number_of - 1) // 2
    giver, receiver = lengths[1:1 + 2 * pairs:2], lengths[2:2 + 2 * pairs:2]
    room = jnp.minimum(giver - 1, limit - receiver)
    moved = jax.random.randint(jax.random.fold_in(stream_key, 1), (pairs,), 0, 1 << 20) % (room + 1)
    lengths = lengths.at[1:1 + 2 * pairs:2].set(giver - moved).at[2:2 + 2 * pairs:2].set(receiver + moved)
    return lengths[jax.random.permutation(jax.random.fold_in(stream_key, 2), number_of)]


def gaussian(own_key, extent, scale, bound, shards=(), dtype=jnp.bfloat16):
    array = jax.random.normal(own_key, extent, jnp.float32) * scale
    if len(shards) > 0:
        array = block_scale(own_key, extent, shards, -0.22, 0.18) * array
    return jnp.clip(array, min=-bound, max=bound).astype(dtype)


def setup_inputs(seed: int = 0) -> dict:
    keys = jax.random.split(jax.random.key(seed), 13)
    tokens = gaussian(keys[0], (NSEQ, LEN, D), 1.0, 6.0, ((0, 4), (1, 4)))
    segments = jax.vmap(lambda own: jnp.searchsorted(jnp.cumsum(ragged_sizes(own, max(4, LEN // 256), LEN, LEN * 3 // 8, 1)), jnp.arange(LEN), side="right"))(jax.random.split(keys[1], NSEQ)).reshape((NSEQ, LEN)).astype(jnp.int32)
    cotangent = gaussian(keys[2], (NSEQ, LEN, D), 1.0, 6.0, ((0, 4), (1, 4)))
    w_qkv = gaussian(keys[3], (D, 3, D), D ** -0.5, 0.21875, ((0, 4), (2, 2)))
    w_out = gaussian(keys[4], (D, D), (D // 64) ** -0.5, 1.75, ((0, 4), (1, 2)))
    w_gate = gaussian(keys[5], (D, FF), D ** -0.5, 0.21875, ((0, 4), (1, 2)))
    w_up = gaussian(keys[6], (D, FF), D ** -0.5, 0.21875, ((0, 4), (1, 2)))
    w_down = gaussian(keys[7], (D, FF), FF ** -0.5, 0.109375, ((0, 4), (1, 2)))
    norm_gain = jnp.clip(1.0 + 0.1 * jax.random.normal(keys[8], (D,), jnp.float32), 0.5, 1.5).astype(jnp.bfloat16)
    norm_bias = gaussian(keys[9], (D,), 0.5, 3.0, ((0, 4),))
    final_gain = jnp.clip(1.0 + 0.1 * jax.random.normal(keys[10], (D,), jnp.float32), 0.5, 1.5).astype(jnp.bfloat16)
    final_bias = gaussian(keys[11], (D,), 0.5, 3.0, ((0, 4),))
    return dict(tokens=tokens, segments=segments, cotangent=cotangent, w_qkv=w_qkv, w_out=w_out, w_gate=w_gate, w_up=w_up, w_down=w_down, norm_gain=norm_gain, norm_bias=norm_bias, final_gain=final_gain, final_bias=final_bias)


@jax.custom_vjp
def low(v):
    return lax.optimization_barrier(v.astype(jnp.bfloat16)).astype(jnp.float32)

@jax.custom_vjp
def low_back(v):
    return v

def low_keep(v):
    return (low(v), None)

def low_pass(kept, grad):
    return (grad,)

def back_keep(v):
    return (v, None)

def back_low(kept, grad):
    return (low(grad),)
low.defvjp(low_keep, low_pass)
low_back.defvjp(back_keep, back_low)
epsilon = 1e-12
rotary_base = 1000.0

def rotary_tables(length, head_size):
    half_size = head_size // 2
    places = jnp.arange(length).astype(jnp.float32)
    inverse = rotary_base ** (-(jnp.arange(half_size).astype(jnp.float32) * 2.0 / head_size))
    angles = places[:, None] * inverse[None, :]
    angles = jnp.concatenate([angles, angles], axis=1)
    return (jnp.cos(angles), jnp.sin(angles))

def rotate_pairs(vector, cosine, sine_t):
    half_size = vector.shape[-1] // 2
    turned = jnp.concatenate([-vector[..., half_size:], vector[..., :half_size]], axis=-1)
    return vector * cosine[:, None, :] + turned * sine_t[:, None, :]

def layer_norm(values, gain_v, bias_v):
    average = lax.optimization_barrier(jnp.mean(values, -1, keepdims=True))
    centred = values - average
    return centred * lax.rsqrt(lax.optimization_barrier(jnp.mean(centred * centred, -1, keepdims=True)) + epsilon) * gain_v + bias_v

def block_layer(params, inputs, doc_ids):
    w_qkv, w_out, w_gate, w_up, w_down, gain_one, bias_one, gain_two, bias_two = params
    highest = lax.Precision.HIGHEST
    length = inputs.shape[0]
    mixed_qkv = low_back(jnp.einsum('td,dcn->tcn', inputs, w_qkv, precision=highest))
    pieces = mixed_qkv.reshape(length, 3, H, HD)
    cosine, sine_t = rotary_tables(length, HD)
    queries = low(rotate_pairs(pieces[:, 0], cosine, sine_t))
    keys_rot = low(rotate_pairs(pieces[:, 1], cosine, sine_t))
    valued = low(pieces[:, 2])
    same_doc = doc_ids[:, None] == doc_ids[None, :]
    factor = HD ** (-0.5)

    def per_head(blocks):
        query_head, key_head, value_head = blocks
        scores = low_back(jnp.dot(query_head, key_head.T, precision=highest) * factor)
        scores = jnp.where(same_doc, scores, -1e+30)
        chances = jax.nn.softmax(scores, axis=-1)
        return low_back(jnp.dot(low(chances), value_head, precision=highest))
    mixture = lax.map(jax.checkpoint(per_head), (queries.transpose(1, 0, 2), keys_rot.transpose(1, 0, 2), valued.transpose(1, 0, 2)))
    mixture = low(mixture.transpose(1, 0, 2).reshape(length, H * HD))
    attended = low_back(jnp.dot(mixture, w_out.T, precision=highest))
    normed = layer_norm(inputs + attended, gain_one, bias_one)
    normed_low = low(normed)
    gate_pre = low_back(jnp.dot(normed_low, w_gate, precision=highest))
    up_pre = low_back(jnp.dot(normed_low, w_up, precision=highest))
    hidden = low(jax.nn.silu(gate_pre) * up_pre)
    branch = low_back(jnp.dot(hidden, w_down.T, precision=highest))
    return layer_norm(normed + branch, gain_two, bias_two)

def reference(tokens, segments, cotangent, w_qkv, w_out, w_gate, w_up, w_down, norm_gain, norm_bias, final_gain, final_bias):
    params = tuple((p.astype(jnp.float32) for p in (w_qkv, w_out, w_gate, w_up, w_down, norm_gain, norm_bias, final_gain, final_bias)))

    def per_sequence(running, blocks):
        inputs, doc_ids, grad_out = blocks

        def forward_fn(weights, values):
            return block_layer(weights, values, doc_ids)
        output, pull_back = jax.vjp(forward_fn, params, inputs.astype(jnp.float32))
        dweights, dinputs = pull_back(grad_out.astype(jnp.float32))
        running = jax.tree.map(jnp.add, running, dweights)
        return (running, (output.astype(jnp.bfloat16), dinputs.astype(jnp.bfloat16)))
    zero_grads = jax.tree.map(jnp.zeros_like, params)
    running, (outputs, dinputs) = lax.scan(per_sequence, zero_grads, (tokens, segments, cotangent))
    return (outputs, dinputs, running[0], running[1], running[2], running[3], running[4], running[5], running[6], running[7], running[8])
```

```python
import functools

import jax
import jax.numpy as jnp
from jax import lax
from jax.experimental import pallas as pl
from jax.experimental.pallas import tpu as pltpu
from jax.sharding import PartitionSpec as P

HD = 64
LONGEST = 768
TILE = 256

epsilon = 1e-12
rotary_base = 1000.0
NEG = -1e30
LOG2E = 1.4426950408889634


bf16 = jnp.bfloat16
f32 = jnp.float32


def xor_perm(count, bit):
    return [(i, i ^ bit) for i in range(count)]


def shift_perm(count, by):
    return [(i, i + by) for i in range(count) if 0 <= i + by < count]


def reorder(values, count, me):
    width = values.shape[-1]
    lead = values.shape[:-1]
    bit, step = 1, width // count
    while bit < count:
        parts = values.reshape(lead + (width // (2 * bit * step), 2, bit * step))
        turned = jnp.concatenate([parts[..., 1:, :], parts[..., :1, :]], axis=-2).reshape(values.shape)
        values = jnp.where((me & bit) != 0, turned, values)
        bit *= 2
    return values


def gather_rows(own, count):
    if count == 4:
        half = own.shape[0] // 2
        near = lax.ppermute(own, "dp", xor_perm(4, 1))
        far = lax.ppermute(own, "dp", xor_perm(4, 2))
        top = lax.ppermute(near[:half], "dp", xor_perm(4, 2))
        low = lax.ppermute(far[half:], "dp", xor_perm(4, 1))
        return jnp.concatenate([own, near, far, top, low], axis=0)
    bit = 1
    while bit < count:
        own = jnp.concatenate([own, lax.ppermute(own, "dp", xor_perm(count, bit))], axis=0)
        bit *= 2
    return own


def scatter_rows(grad, count):
    rows = grad.shape[0] // count
    if count == 4:
        half = rows // 2
        cut = lambda first, last: grad[first:last].astype(bf16)
        b1a, b1b = (rows, rows + half), (rows + half, 2 * rows)
        b2a, b2b = (2 * rows, 2 * rows + half), (2 * rows + half, 3 * rows)
        b3a, b3b = (3 * rows, 3 * rows + half), (3 * rows + half, 4 * rows)
        x_first = lax.ppermute(jnp.concatenate([cut(*b3a), cut(*b1a)], 0), "dp", xor_perm(4, 1))
        y_first = lax.ppermute(jnp.concatenate([cut(*b3b), cut(*b2b)], 0), "dp", xor_perm(4, 2))
        x_next = (grad[b1b[0] : b1b[1]].astype(f32) + y_first[:half].astype(f32)).astype(bf16)
        y_next = (grad[b2a[0] : b2a[1]].astype(f32) + x_first[:half].astype(f32)).astype(bf16)
        x_last = lax.ppermute(x_next, "dp", xor_perm(4, 1))
        y_last = lax.ppermute(y_next, "dp", xor_perm(4, 2))
        first = grad[:half].astype(f32) + x_first[half:].astype(f32) + y_last.astype(f32)
        second = grad[half:rows].astype(f32) + y_first[half:].astype(f32) + x_last.astype(f32)
        return jnp.concatenate([first, second], 0)
    grad, total = grad.astype(f32), count
    while count > 1:
        count //= 2
        keep = count * rows
        got = lax.ppermute(grad[keep:].astype(bf16), "dp", xor_perm(total, count))
        grad = grad[:keep] + got.astype(f32)
    return grad


def total_over_ctx(part, count, me):
    rows = part.shape[0] // count
    low = part.astype(bf16)
    piece = lambda which: lax.dynamic_slice_in_dim(low, which * rows, rows, 0)
    summed = piece(me).astype(f32)
    for k in range(1, count):
        summed = summed + lax.ppermute(piece(me ^ k), "ctx", xor_perm(count, k)).astype(f32)
    mine = summed.astype(bf16)
    out = jnp.zeros(part.shape, f32)
    out = lax.dynamic_update_slice_in_dim(out, mine.astype(f32), me * rows, 0)
    for k in range(1, count):
        got = lax.ppermute(mine, "ctx", xor_perm(count, k))
        out = lax.dynamic_update_slice_in_dim(out, got.astype(f32), (me ^ k) * rows, 0)
    return out


def total_small(part, count_dp, count_ctx, me_dp):
    width = part.shape[1]
    size = width // count_dp
    live = count_dp
    while live > 1:
        live //= 2
        got = lax.ppermute(part[:, live * size :], "dp", xor_perm(count_dp, live))
        part = part[:, : live * size] + got
    bit = 1
    while bit < count_ctx:
        part = part + lax.ppermute(part, "ctx", xor_perm(count_ctx, bit))
        bit *= 2
    return part


def add_over_tp(part, count):
    low = part.astype(bf16)
    bit = 1
    total = low
    while bit < count:
        got = lax.ppermute(total, "tp", xor_perm(count, bit))
        total = total.astype(f32) + got.astype(f32)
        bit *= 2
    return total.astype(f32)


def turn(values, cosine, sine_a, sine_b):
    width = values.shape[-1]
    ahead = pltpu.roll(values, width - HD // 2, 1)
    behind = pltpu.roll(values, HD // 2, 1)
    return values * cosine + ahead * sine_a + behind * sine_b


def project_kernel(own_ref, left_ref, right_ref, w_ref, cos_ref, sa_ref, sb_ref, q_ref, k_ref, v_ref, *, first, last):
    block = pl.program_id(1)
    width = k_ref.shape[2]
    cosine, sine_a, sine_b = cos_ref[...], sa_ref[...], sb_ref[...]

    def emit(rows, with_query):
        for kind, ref in ((0, q_ref), (1, k_ref), (2, v_ref)):
            if kind == 0 and not with_query:
                continue
            out = jnp.dot(rows, w_ref[:, kind * width : (kind + 1) * width], preferred_element_type=f32)
            if kind == 2:
                ref[0] = out.astype(bf16)
            else:
                for at in range(0, width, 128):
                    ref[0, :, at : at + 128] = turn(out[:, at : at + 128], cosine, sine_a, sine_b).astype(bf16)

    @pl.when(block < first)
    def _():
        emit(left_ref[0], False)

    @pl.when((block >= first) & (block < last))
    def _():
        emit(own_ref[0], True)

    @pl.when(block >= last)
    def _():
        emit(right_ref[0], False)


def project(own, left, right, weight, cosine, sine_a, sine_b):
    seqs, rows, width = own.shape
    halo = left.shape[1]
    local = weight.shape[1] // 3
    window = 2 * halo + rows
    first, blocks = halo // TILE, window // TILE
    last = first + rows // TILE
    own_at = lambda s, b: (s, jnp.clip(b - first, 0, last - first - 1), 0)
    left_at = lambda s, b: (s, jnp.minimum(b, first - 1), 0)
    right_at = lambda s, b: (s, jnp.clip(b - last, 0, blocks - last - 1), 0)
    table = pl.BlockSpec((TILE, 128), lambda s, b: (b, 0))
    return pl.pallas_call(
        functools.partial(project_kernel, first=first, last=last),
        grid=(seqs, blocks),
        in_specs=[
            pl.BlockSpec((1, TILE, width), own_at),
            pl.BlockSpec((1, TILE, width), left_at),
            pl.BlockSpec((1, TILE, width), right_at),
            pl.BlockSpec(weight.shape, lambda s, b: (0, 0)),
            table,
            table,
            table,
        ],
        out_specs=[
            pl.BlockSpec((1, TILE, local), own_at),
            pl.BlockSpec((1, TILE, local), lambda s, b: (s, b, 0)),
            pl.BlockSpec((1, TILE, local), lambda s, b: (s, b, 0)),
        ],
        out_shape=[
            jax.ShapeDtypeStruct((seqs, rows, local), bf16),
            jax.ShapeDtypeStruct((seqs, window, local), bf16),
            jax.ShapeDtypeStruct((seqs, window, local), bf16),
        ],
        cost_estimate=pl.CostEstimate(
            flops=2 * seqs * window * width * 2 * local, transcendentals=0, bytes_accessed=16 << 20
        ),
        name="project",
    )(own, left, right, weight, cosine, sine_a, sine_b)


def head_lanes(values, head):
    lane = lax.broadcasted_iota(jnp.int32, values.shape, 1)
    inside = (lane < HD) if head == 0 else (lane >= HD)
    return jnp.where(inside, values, jnp.zeros_like(values))


def across(left, right):
    return lax.dot_general(left, right, (((1,), (1,)), ((), ())), preferred_element_type=f32)


def attend_kernel(span_ref, q_ref, k_ref, v_ref, sk_ref, sq_ref, o_ref, l_ref):
    seq = pl.program_id(0)
    rows = q_ref.shape[1]
    scale = HD**-0.5 * LOG2E
    for blk in range(rows // TILE):
        at = blk * TILE
        query = q_ref[0, at : at + TILE, :]
        queries = [head_lanes(query, h) for h in range(2)]
        seg_q = sq_ref[0, 0:1, at : at + TILE]

        def step(j, carry):
            start = pl.multiple_of(j * TILE, TILE)
            keys = k_ref[0, pl.ds(start, TILE), :]
            turned = v_ref[0, pl.ds(start, TILE), :].T
            seg_k = sk_ref[0, pl.ds(start, TILE), :]
            same = jnp.concatenate([seg_k] * (TILE // 128), 1) == seg_q
            out = []
            for h in range(2):
                largest, total, acc = carry[h]
                scores = jnp.where(same, across(keys, queries[h]) * scale, NEG)
                bigger = jnp.maximum(largest, jnp.max(scores, 0, keepdims=True))
                probs = jnp.exp2(scores - bigger)
                shrink = jnp.exp2(largest - bigger)
                total = total * shrink + jnp.sum(probs, 0, keepdims=True)
                acc = acc * shrink + jnp.dot(
                    turned[h * HD : (h + 1) * HD], probs.astype(bf16), preferred_element_type=f32
                )
                out.append((bigger, total, acc))
            return tuple(out)

        fresh = (
            jnp.full((1, TILE), NEG, f32),
            jnp.zeros((1, TILE), f32),
            jnp.zeros((HD, TILE), f32),
        )
        low, high = span_ref[seq, 2 * blk], span_ref[seq, 2 * blk + 1]
        done = lax.fori_loop(low, high, step, (fresh, fresh))
        parts = []
        for h in range(2):
            largest, total, acc = done[h]
            parts.append(acc / total)
            l_ref[0, 0, h : h + 1, at : at + TILE] = largest + jnp.log2(total)
        o_ref[0, at : at + TILE, :] = jnp.concatenate(parts, 0).T.astype(bf16)


def attend(span, q, k, v, seg_k, seg_q):
    seqs, rows, local = q.shape
    window = k.shape[1]
    pairs = local // 128
    whole = lambda size: pl.BlockSpec((1, size, 128), lambda s, p, span: (s, 0, p))
    return pl.pallas_call(
        attend_kernel,
        grid_spec=pltpu.PrefetchScalarGridSpec(
            num_scalar_prefetch=1,
            grid=(seqs, pairs),
            in_specs=[
                whole(rows),
                whole(window),
                whole(window),
                pl.BlockSpec((1, window, 128), lambda s, p, span: (s, 0, 0)),
                pl.BlockSpec((1, 8, rows), lambda s, p, span: (s, 0, 0)),
            ],
            out_specs=[
                whole(rows),
                pl.BlockSpec((1, 1, 2, rows), lambda s, p, span: (s, p, 0, 0)),
            ],
        ),
        out_shape=[
            jax.ShapeDtypeStruct((seqs, rows, local), bf16),
            jax.ShapeDtypeStruct((seqs, pairs, 2, rows), f32),
        ],
        cost_estimate=pl.CostEstimate(flops=8 << 30, transcendentals=8 << 20, bytes_accessed=8 << 20),
        name="attend",
    )(span, q, k, v, seg_k, seg_q)


def attend_back_kernel(
    span_ref, q_ref, k_ref, v_ref, sk_ref, sq_ref, o_ref, l_ref, g_ref, cos_ref, sa_ref, sb_ref,
    dq_ref, dk_ref, dv_ref, dk_acc, dv_acc, *, first
):
    seq = pl.program_id(0)
    rows = q_ref.shape[1]
    window = k_ref.shape[1]
    factor = HD**-0.5
    scale = factor * LOG2E
    dk_acc[...] = jnp.zeros_like(dk_acc)
    dv_acc[...] = jnp.zeros_like(dv_acc)
    for blk in range(rows // TILE):
        at = blk * TILE
        query = q_ref[0, at : at + TILE, :]
        grad = g_ref[0, at : at + TILE, :]
        queries = [head_lanes(query, h) for h in range(2)]
        grads = [head_lanes(grad, h) for h in range(2)]
        product = (grad.astype(f32) * o_ref[0, at : at + TILE, :].astype(f32)).T
        deltas = [jnp.sum(product[h * HD : (h + 1) * HD], 0, keepdims=True) for h in range(2)]
        logs = [l_ref[0, 0, h : h + 1, at : at + TILE] for h in range(2)]
        seg_q = sq_ref[0, 0:1, at : at + TILE]

        def step(j, carry):
            start = pl.multiple_of(j * TILE, TILE)
            keys = k_ref[0, pl.ds(start, TILE), :]
            vals = v_ref[0, pl.ds(start, TILE), :]
            turned = keys.T
            seg_k = sk_ref[0, pl.ds(start, TILE), :]
            same = jnp.concatenate([seg_k] * (TILE // 128), 1) == seg_q
            out = []
            dv = dv_acc[pl.ds(start, TILE), :]
            dk = dk_acc[pl.ds(start, TILE), :]
            for h in range(2):
                scores = jnp.where(same, across(keys, queries[h]) * scale, NEG)
                probs = jnp.exp2(scores - logs[h])
                dprobs = across(vals, grads[h])
                dscores = (probs * (dprobs - deltas[h])).astype(bf16)
                dv = dv + jnp.dot(probs.astype(bf16), grads[h], preferred_element_type=f32)
                dk = dk + jnp.dot(dscores, queries[h], preferred_element_type=f32)
                out.append(
                    carry[h]
                    + jnp.dot(turned[h * HD : (h + 1) * HD], dscores, preferred_element_type=f32)
                )
            dv_acc[pl.ds(start, TILE), :] = dv
            dk_acc[pl.ds(start, TILE), :] = dk
            return tuple(out)

        fresh = jnp.zeros((HD, TILE), f32)
        low, high = span_ref[seq, 2 * blk], span_ref[seq, 2 * blk + 1]
        done = lax.fori_loop(low, high, step, (fresh, fresh))
        dq = jnp.concatenate(done, 0).T * factor
        row = first + at
        dq_ref[0, at : at + TILE, :] = turn(
            dq, cos_ref[row : row + TILE, :], -sa_ref[row : row + TILE, :], -sb_ref[row : row + TILE, :]
        ).astype(bf16)
    for at in range(0, window, TILE):
        dk = dk_acc[at : at + TILE, :] * factor
        dk_ref[0, at : at + TILE, :] = turn(
            dk, cos_ref[at : at + TILE, :], -sa_ref[at : at + TILE, :], -sb_ref[at : at + TILE, :]
        ).astype(bf16)
        dv_ref[0, at : at + TILE, :] = dv_acc[at : at + TILE, :].astype(bf16)


def attend_back(span, q, k, v, seg_k, seg_q, out, logs, grad, cosine, sine_a, sine_b):
    seqs, rows, local = q.shape
    window = k.shape[1]
    pairs = local // 128
    whole = lambda size: pl.BlockSpec((1, size, 128), lambda s, p, span: (s, 0, p))
    table = pl.BlockSpec((window, 128), lambda s, p, span: (0, 0))
    return pl.pallas_call(
        functools.partial(attend_back_kernel, first=(window - rows) // 2),
        grid_spec=pltpu.PrefetchScalarGridSpec(
            num_scalar_prefetch=1,
            grid=(seqs, pairs),
            in_specs=[
                whole(rows),
                whole(window),
                whole(window),
                pl.BlockSpec((1, window, 128), lambda s, p, span: (s, 0, 0)),
                pl.BlockSpec((1, 8, rows), lambda s, p, span: (s, 0, 0)),
                whole(rows),
                pl.BlockSpec((1, 1, 2, rows), lambda s, p, span: (s, p, 0, 0)),
                whole(rows),
                table,
                table,
                table,
            ],
            out_specs=[whole(rows), whole(window), whole(window)],
            scratch_shapes=[pltpu.VMEM((window, 128), f32), pltpu.VMEM((window, 128), f32)],
        ),
        out_shape=[
            jax.ShapeDtypeStruct((seqs, rows, local), bf16),
            jax.ShapeDtypeStruct((seqs, window, local), bf16),
            jax.ShapeDtypeStruct((seqs, window, local), bf16),
        ],
        cost_estimate=pl.CostEstimate(flops=24 << 30, transcendentals=8 << 20, bytes_accessed=16 << 20),
        name="attend_back",
    )(span, q, k, v, seg_k, seg_q, out, logs, grad, cosine, sine_a, sine_b)


def norm_forward(values, gain_v, bias_v):
    average = jnp.mean(values, -1, keepdims=True)
    centred = values - average
    inv_std = lax.rsqrt(jnp.mean(centred * centred, -1, keepdims=True) + epsilon)
    unit_v = centred * inv_std
    return (unit_v * gain_v + bias_v, unit_v, inv_std)


def norm_backward(gradient, unit_v, inv_std, gain_v):
    scaled = gradient * gain_v
    dvalues = (
        scaled
        - jnp.mean(scaled, -1, keepdims=True)
        - unit_v * jnp.mean(scaled * unit_v, -1, keepdims=True)
    ) * inv_std
    return (dvalues, jnp.sum(gradient * unit_v, 0), jnp.sum(gradient, 0))


def contract_rows(left, right):
    return lax.dot_general(left, right, (((0,), (0,)), ((), ())), preferred_element_type=f32)


def contract_cols(left, right):
    return lax.dot_general(left, right, (((1,), (1,)), ((), ())), preferred_element_type=f32)


def halves(values, count, me):
    width = values.shape[-1] // count
    return lambda which: lax.dynamic_slice_in_dim(values, which * width, width, values.ndim - 1)


def join_tp(mine, other, me):
    return jnp.where(me == 0, jnp.concatenate([mine, other], -1), jnp.concatenate([other, mine], -1))


def reach(rows):
    left, out, far = LONGEST, [], 1
    while left > 0:
        out.append((far, min(rows, left)))
        left -= rows
        far += 1
    return out


def body(sizes, tokens, segments, cotangent, w_qkv, w_out, w_gate, w_up, w_down, norm_gain, norm_bias, final_gain, final_bias):
    n_dp, n_ctx, n_tp = sizes
    me_dp, me_ctx, me_tp = lax.axis_index("dp"), lax.axis_index("ctx"), lax.axis_index("tp")
    seqs, rows, width = tokens.shape
    count = seqs * rows
    local = w_qkv.shape[2]
    window = rows + 2 * LONGEST

    qkv_w = gather_rows(w_qkv.reshape(w_qkv.shape[0], 3 * local), n_dp)
    x = reorder(tokens, n_dp, me_dp)

    send = lax.dynamic_slice_in_dim(x, me_tp * (width // n_tp), width // n_tp, 2)
    marks = segments + 1
    left_x, right_x, left_s, right_s = [], [], [], []
    for far, take in reach(rows):
        left_x.insert(0, lax.ppermute(send[:, rows - take :], "ctx", shift_perm(n_ctx, far)))
        right_x.append(lax.ppermute(send[:, :take], "ctx", shift_perm(n_ctx, -far)))
        left_s.insert(0, lax.ppermute(marks[:, rows - take :], "ctx", shift_perm(n_ctx, far)))
        right_s.append(lax.ppermute(marks[:, :take], "ctx", shift_perm(n_ctx, -far)))
    share = jnp.concatenate(left_x + right_x, 1)
    other = lax.ppermute(share, "tp", xor_perm(n_tp, 1))
    beside = join_tp(share, other, me_tp)
    left, right = beside[:, :LONGEST], beside[:, LONGEST:]
    marks_all = jnp.concatenate(left_s + [marks] + right_s, 1)

    out_w = gather_rows(w_out, n_dp)
    params = gather_rows(jnp.stack([norm_gain, norm_bias, final_gain, final_bias], 1), n_dp).astype(f32).T
    gain_one, bias_one, gain_two, bias_two = params[0], params[1], params[2], params[3]
    gate_w = gather_rows(w_gate, n_dp)
    up_w = gather_rows(w_up, n_dp)
    down_w = gather_rows(w_down, n_dp)

    half = HD // 2
    places = (me_ctx * rows - LONGEST + jnp.arange(window)).astype(f32)
    inverse = rotary_base ** (-(jnp.arange(half).astype(f32) * 2.0 / HD))
    angles = places[:, None] * inverse[None, :]
    cosine, sine = jnp.cos(angles), jnp.sin(angles)
    none = jnp.zeros_like(sine)
    cos_t = jnp.concatenate([cosine] * 4, 1)
    sin_a = jnp.concatenate([-sine, none] * 2, 1)
    sin_b = jnp.concatenate([none, sine] * 2, 1)
    seg_k = jnp.broadcast_to(marks_all[:, :, None], (seqs, window, 128))
    seg_q = jnp.broadcast_to(marks[:, None, :], (seqs, 8, rows))
    spans = []
    in_block = marks_all.reshape(seqs, window // TILE, TILE)
    order = jnp.arange(window // TILE)
    for blk in range(rows // TILE):
        lowest, highest = marks[:, blk * TILE], marks[:, (blk + 1) * TILE - 1]
        hit = jnp.any((in_block >= lowest[:, None, None]) & (in_block <= highest[:, None, None]), -1)
        spans.append(jnp.min(jnp.where(hit, order, window), 1))
        spans.append(jnp.max(jnp.where(hit, order, -1), 1) + 1)
    span = jnp.stack(spans, 1).astype(jnp.int32)

    q, k, v = project(x, left, right, qkv_w, cos_t, sin_a, sin_b)
    mixture, logs = attend(span, q, k, v, seg_k, seg_q)

    flat = x.reshape(count, width)
    mixture_flat = mixture.reshape(count, local)
    attended = add_over_tp(contract_cols(mixture_flat, out_w), n_tp)
    normed, unit_one, inv_one = norm_forward(flat.astype(f32) + attended, gain_one, bias_one)
    normed_low = normed.astype(bf16)
    gate_pre = jnp.dot(normed_low, gate_w, preferred_element_type=f32)
    up_pre = jnp.dot(normed_low, up_w, preferred_element_type=f32)
    sigmoid_g = jax.nn.sigmoid(gate_pre)
    activated = gate_pre * sigmoid_g
    hidden_low = (activated * up_pre).astype(bf16)
    branch = add_over_tp(contract_cols(hidden_low, down_w), n_tp)
    final_out, unit_two, inv_two = norm_forward(normed + branch, gain_two, bias_two)
    output = reorder(final_out.astype(bf16), n_dp, me_dp).reshape(seqs, rows, width)

    grad_out = reorder(cotangent, n_dp, me_dp).reshape(count, width).astype(f32)
    dsum, dgain_two, dbias_two = norm_backward(grad_out, unit_two, inv_two, gain_two)
    dbranch = dsum.astype(bf16)
    d_down = contract_rows(dbranch, hidden_low).astype(bf16)
    dhidden = jnp.dot(dbranch, down_w, preferred_element_type=f32)
    dgate = (dhidden * up_pre * sigmoid_g * (1.0 + gate_pre * (1.0 - sigmoid_g))).astype(bf16)
    dup = (dhidden * activated).astype(bf16)
    dnormed_part = contract_cols(dgate, gate_w) + contract_cols(dup, up_w)
    dnormed = dsum + add_over_tp(dnormed_part, n_tp)
    d_gate = contract_rows(normed_low, dgate).astype(bf16)
    d_up = contract_rows(normed_low, dup).astype(bf16)
    dresid, dgain_one, dbias_one = norm_backward(dnormed, unit_one, inv_one, gain_one)
    dattended = dresid.astype(bf16)
    d_out = contract_rows(dattended, mixture_flat).astype(bf16)
    dmixture = jnp.dot(dattended, out_w, preferred_element_type=f32).astype(bf16).reshape(seqs, rows, local)

    def reduced(grad):
        return total_over_ctx(scatter_rows(grad, n_dp), n_ctx, me_ctx)

    g_down = reduced(d_down)
    g_gate = reduced(d_gate)
    g_up = reduced(d_up)
    small = total_small(jnp.stack([dgain_one, dbias_one, dgain_two, dbias_two]), n_dp, n_ctx, me_dp)

    dq, dk, dv = attend_back(span, q, k, v, seg_k, seg_q, mixture, logs, dmixture, cos_t, sin_a, sin_b)

    w_q, w_kv = qkv_w[:, :local], qkv_w[:, local:]
    dkv = jnp.concatenate([dk, dv], 2)
    back = lambda grad, weight: lax.dot_general(grad, weight, (((2,), (1,)), ((), ())), preferred_element_type=f32)
    dx = back(dkv, w_kv)
    dx_own = dx[:, LONGEST : LONGEST + rows] + back(dq, w_q)
    dx = jnp.concatenate([dx[:, :LONGEST], dx_own, dx[:, LONGEST + rows :]], 1).astype(bf16)
    share_of = halves(dx, n_tp, me_tp)
    dx_half = share_of(me_tp).astype(f32) + lax.ppermute(share_of(1 - me_tp), "tp", xor_perm(n_tp, 1)).astype(f32)
    dx_low = dx_half.astype(bf16)
    total = dx_half[:, LONGEST : LONGEST + rows]
    at = LONGEST
    for far, take in reach(rows):
        to_left = dx_low[:, at - take : at]
        to_right = dx_low[:, window - at : window - at + take]
        from_right = lax.ppermute(to_left, "ctx", shift_perm(n_ctx, -far)).astype(f32)
        from_left = lax.ppermute(to_right, "ctx", shift_perm(n_ctx, far)).astype(f32)
        pad = rows - take
        total = total + jnp.pad(from_right, ((0, 0), (pad, 0), (0, 0))) + jnp.pad(from_left, ((0, 0), (0, pad), (0, 0)))
        at -= take
    mine = total.astype(bf16)
    dinput = join_tp(mine, lax.ppermute(mine, "tp", xor_perm(n_tp, 1)), me_tp).reshape(count, width)
    d_tokens = reorder((dresid + dinput.astype(f32)).astype(bf16), n_dp, me_dp).reshape(seqs, rows, width)

    x_window = jnp.concatenate([left, x, right], 1).reshape(seqs * window, width)
    d_q = contract_rows(flat, dq.reshape(count, local))
    d_kv = contract_rows(x_window, dkv.reshape(seqs * window, 2 * local))
    d_last = jnp.concatenate([d_q.astype(bf16), d_kv.astype(bf16), d_out], 1)
    g_last = reduced(d_last)
    g_qkv = g_last[:, : 3 * local].reshape(g_last.shape[0], 3, local)
    g_out = g_last[:, 3 * local :]
    return (output, d_tokens, g_qkv, g_out, g_gate, g_up, g_down, small[0], small[1], small[2], small[3])


def solution(mesh):
    sizes = (mesh.shape["dp"], mesh.shape["ctx"], mesh.shape["tp"])
    wide, flat, kinds, square, line = (
        P("dp", "ctx", None),
        P("dp", "ctx"),
        P("dp", None, "tp"),
        P("dp", "tp"),
        P("dp"),
    )
    return jax.shard_map(
        functools.partial(body, sizes),
        mesh=mesh,
        in_specs=(wide, flat, wide, kinds) + (square,) * 4 + (line,) * 4,
        out_specs=(wide, wide, kinds) + (square,) * 4 + (line,) * 4,
        check_vma=False,
    )
```

```python
import functools

import jax
import jax.numpy as jnp
from jax import lax
from jax.experimental import pallas as pl
from jax.experimental.pallas import tpu as pltpu
from jax.sharding import PartitionSpec as P

HD = 64
LONGEST = 768
TILE = 256

epsilon = 1e-12
rotary_base = 1000.0
NEG = -1e30
LOG2E = 1.4426950408889634


bf16 = jnp.bfloat16
f32 = jnp.float32


def xor_perm(count, bit):
    return [(i, i ^ bit) for i in range(count)]


def shift_perm(count, by):
    return [(i, i + by) for i in range(count) if 0 <= i + by < count]


def sent(values, axis, perm):
    return lax.ppermute(values, axis, perm)


def move(copies, sources, shapes, scalars, name):
    count = len(sources)

    def kernel(scalar_ref, *refs):
        given, made, sems = refs[:count], refs[count:-1], refs[-1]
        started = []
        for n, (src, src_at, dst, dst_at) in enumerate(copies):
            copy = pltpu.make_async_copy(
                given[src].at[src_at(scalar_ref)], made[dst].at[dst_at(scalar_ref)], sems.at[n]
            )
            copy.start()
            started.append(copy)
        for copy in started:
            copy.wait()

    anywhere = pl.BlockSpec(memory_space=pl.ANY)
    return pl.pallas_call(
        kernel,
        grid_spec=pltpu.PrefetchScalarGridSpec(
            num_scalar_prefetch=1,
            grid=(),
            in_specs=[anywhere] * count,
            out_specs=[anywhere] * len(shapes),
            scratch_shapes=[pltpu.SemaphoreType.DMA((len(copies),))],
        ),
        out_shape=[jax.ShapeDtypeStruct(shape, bf16) for shape in shapes],
        name=name,
    )(scalars, *sources)


def rows_at(index, start, size):
    return lambda ref: (pl.ds(pl.multiple_of(ref[index] * start[0] + start[1], 16), size), slice(None))


def all_rows(*cols):
    cut = slice(*cols) if cols else slice(None)
    return lambda ref: (slice(None), cut)


def fetch_rows(own, after=None):
    half = own.shape[0] // 2
    near = sent(own, "dp", xor_perm(4, 1))
    far = sent(own, "dp", xor_perm(4, 2))
    top = sent(near[:half], "dp", xor_perm(4, 2))
    low = sent(far[half:], "dp", xor_perm(4, 1))
    return near, far, top, low


def gather_rows(own, me, count):
    bit = 1
    while bit < count:
        got = sent(own, "dp", xor_perm(count, bit))
        own = jnp.where((me & bit) != 0, jnp.concatenate([got, own], 0), jnp.concatenate([own, got], 0))
        bit *= 2
    return own


def scatter_rows(grad, me, count):
    bit, grad = count // 2, grad.astype(f32)
    while bit >= 1:
        half = grad.shape[0] // 2
        side = jnp.where((me & bit) != 0, 1, 0)
        give = lax.dynamic_slice_in_dim(grad, (1 - side) * half, half, 0).astype(bf16)
        grad = lax.dynamic_slice_in_dim(grad, side * half, half, 0)
        grad = grad + sent(give, "dp", xor_perm(count, bit)).astype(f32)
        bit //= 2
    return grad.astype(bf16)


def add_kernel(scalar_ref, *refs, rows, terms, stack):
    made = refs[-1:] if stack else refs[-len(terms) :]
    at = 0
    for n, count in enumerate(terms):
        total = refs[at][...].astype(f32)
        for k in range(1, count):
            total = total + refs[at + k][...].astype(f32)
        if stack:
            made[0][n * rows : (n + 1) * rows] = total.astype(bf16)
        else:
            made[n][...] = total.astype(bf16)
        at += count


def add_blocks(scalars, sums, rows, cols, after, name, stack=False):
    outs, height = (1, rows * len(sums)) if stack else (len(sums), rows)
    specs, values, terms = [], [], []
    step = 512 if cols % 512 == 0 else cols
    for parts in sums:
        terms.append(len(parts))
        for array, index in parts:
            if callable(index):
                at = lambda c, ref, index=index: (index(ref), c)
            else:
                at = lambda c, ref, index=index: (index, c)
            specs.append(pl.BlockSpec((rows, step), at))
            values.append(array)
    anywhere = pl.BlockSpec(memory_space=pl.ANY)
    return pl.pallas_call(
        functools.partial(add_kernel, rows=rows, terms=terms, stack=stack),
        grid_spec=pltpu.PrefetchScalarGridSpec(
            num_scalar_prefetch=1,
            grid=(cols // step,),
            in_specs=specs + [anywhere] * len(after),
            out_specs=[pl.BlockSpec((height, step), lambda c, ref: (0, c))] * outs,
        ),
        out_shape=[jax.ShapeDtypeStruct((height, cols), bf16)] * outs,
        name=name,
    )(scalars, *values, *after)


class Reduction:
    def __init__(self, grad, sizes, mine, scalars, name):
        self.grad, self.name, self.scalars = grad, name, scalars
        self.n_dp, self.n_ctx, _ = sizes
        self.me_dp, self.me_ctx = mine
        self.rows, self.cols = grad.shape[0] // self.n_dp, grad.shape[1]
        self.half = self.rows // 2
        self.direct = self.n_dp == 4 and self.half % 16 == 0

    def first(self):
        if not self.direct:
            self.part = scatter_rows(self.grad, self.me_dp, self.n_dp)
            return self
        rows, half = self.rows, self.half
        cut = lambda k, offset: rows_at(k, (rows, offset), half)
        at = lambda start: lambda ref: (pl.ds(start, half), slice(None))
        x_give, y_give = move(
            [(0, cut(3, 0), 0, at(0)), (0, cut(1, 0), 0, at(half)), (0, cut(3, half), 1, at(0)), (0, cut(2, half), 1, at(half))],
            [self.grad],
            [(rows, self.cols)] * 2,
            self.scalars,
            "pick_" + self.name,
        )
        self.token = x_give
        self.x_got = sent(x_give, "dp", xor_perm(4, 1))
        self.y_got = sent(y_give, "dp", xor_perm(4, 2))
        return self

    def second(self, *after):
        if not self.direct:
            return self
        x_next, y_next = add_blocks(
            self.scalars,
            [
                [(self.grad, lambda ref: ref[1] * 2 + 1), (self.y_got, 0)],
                [(self.grad, lambda ref: ref[2] * 2), (self.x_got, 0)],
            ],
            self.half,
            self.cols,
            after,
            "add_second_" + self.name,
        )
        self.token = x_next
        self.x_last = sent(x_next, "dp", xor_perm(4, 1))
        self.y_last = sent(y_next, "dp", xor_perm(4, 2))
        return self

    def inward(self, *after):
        if self.direct:
            (self.part,) = add_blocks(
                self.scalars,
                [
                    [(self.grad, lambda ref: ref[0] * 2), (self.x_got, 1), (self.y_last, 0)],
                    [(self.grad, lambda ref: ref[0] * 2 + 1), (self.y_got, 1), (self.x_last, 0)],
                ],
                self.half,
                self.cols,
                after,
                "add_inward_" + self.name,
                stack=True,
            )
        if self.n_ctx == 4:
            self.got = sent(self.part, "ctx", [(0, 1), (3, 2)])
        self.token = self.part
        return self

    def plus(self, name, after):
        if self.rows % 16 == 0:
            (self.part,) = add_blocks(
                self.scalars, [[(self.part, 0), (self.got, 0)]], self.rows, self.cols, after, name + self.name
            )
        else:
            self.part = (self.part.astype(f32) + self.got.astype(f32)).astype(bf16)
        self.token = self.part

    def across(self, *after):
        if self.n_ctx == 4:
            self.plus("add_across_", after)
            self.got = sent(self.part, "ctx", [(1, 2), (2, 1)])
        return self

    def outward(self, *after):
        if self.n_ctx == 4:
            self.plus("add_outward_", after)
            self.got = sent(self.part, "ctx", [(1, 0), (2, 3)])
        return self

    def result(self):
        if self.n_ctx == 4:
            edge = (self.me_ctx == 0) | (self.me_ctx == 3)
            return jnp.where(edge, self.got, self.part).astype(f32)
        part, bit = self.part, 1
        while bit < self.n_ctx:
            got = sent(part, "ctx", xor_perm(self.n_ctx, bit))
            part = (part.astype(f32) + got.astype(f32)).astype(bf16)
            bit *= 2
        return part.astype(f32)


def total_small(part, me, sizes):
    n_dp, n_ctx, _ = sizes
    bit = n_dp // 2
    while bit >= 1:
        half = part.shape[1] // 2
        side = jnp.where((me & bit) != 0, 1, 0)
        give = lax.dynamic_slice_in_dim(part, (1 - side) * half, half, 1)
        part = lax.dynamic_slice_in_dim(part, side * half, half, 1) + sent(give, "dp", xor_perm(n_dp, bit))
        bit //= 2
    bit = 1
    while bit < n_ctx:
        part = part + sent(part, "ctx", xor_perm(n_ctx, bit))
        bit *= 2
    return part


def add_over_tp(part, count):
    low = part.astype(bf16)
    bit = 1
    total = low
    while bit < count:
        got = lax.ppermute(total, "tp", xor_perm(count, bit))
        total = total.astype(f32) + got.astype(f32)
        bit *= 2
    return total.astype(f32)


def turn(values, cosine, sine_a, sine_b):
    width = values.shape[-1]
    ahead = pltpu.roll(values, width - HD // 2, 1)
    behind = pltpu.roll(values, HD // 2, 1)
    return values * cosine + ahead * sine_a + behind * sine_b


class Window:
    def __init__(self, seqs, rows, pieces_left, pieces_right):
        self.parts = []
        at = 0
        for kind, sizes in (("left", pieces_left), ("own", [rows]), ("right", pieces_right)):
            for n, size in enumerate(sizes):
                self.parts.append((kind, at, at + size // TILE))
                at += size // TILE
        self.blocks = at
        self.first, self.last = next((lo, hi) for kind, lo, hi in self.parts if kind == "own")

    def own_block(self, b):
        return jnp.clip(b - self.first, 0, self.last - self.first - 1)

    def specs(self, width):
        out = []
        for kind, lo, hi in self.parts:
            at = lambda s, b, *ref, lo=lo, hi=hi: (s, jnp.clip(b - lo, 0, hi - lo - 1), 0)
            if kind == "own":
                out.append(pl.BlockSpec((1, TILE, width), at))
            else:
                out += [pl.BlockSpec((1, TILE, width // 2), at)] * 2
        return out

    def visit(self, refs, block, emit):
        at = 0
        for kind, lo, hi in self.parts:
            mine = refs[at : at + (1 if kind == "own" else 2)]
            at += len(mine)

            @pl.when((block >= lo) & (block < hi))
            def _():
                emit([ref[0] for ref in mine])


def project_kernel(scalar_ref, *refs, shape, pieces, plan):
    rows_in = refs[:pieces]
    weights = refs[pieces : pieces + len(plan)]
    cos_ref, sa_ref, sb_ref, q_ref, k_ref, v_ref, w_ref = refs[pieces + len(plan) :]
    width = k_ref.shape[2]
    core = scalar_ref[4]

    @pl.when((pl.program_id(0) == 0) & (pl.program_id(1) == 0))
    def _():
        for ref, (index, size, offset) in zip(weights, plan):
            rows = ref.shape[0]
            w_ref[pl.ds(pl.multiple_of(scalar_ref[index] * size + offset, 16), rows), :] = ref[...]

    cosine, sine_a, sine_b = cos_ref[...], sa_ref[...], sb_ref[...]

    def emit(parts):
        full = len(parts) == 1
        half = w_ref.shape[0] // 2
        for kind, ref in ((0, q_ref), (1, k_ref), (2, v_ref)):
            if kind == 0 and not full:
                continue
            cols = slice(kind * width, (kind + 1) * width)
            if full:
                out = jnp.dot(parts[0], w_ref[:, cols], preferred_element_type=f32)
            else:
                mine = pl.multiple_of(core * half, 16)
                other = pl.multiple_of((1 - core) * half, 16)
                out = jnp.dot(parts[0], w_ref[pl.ds(mine, half), cols], preferred_element_type=f32)
                out = out + jnp.dot(parts[1], w_ref[pl.ds(other, half), cols], preferred_element_type=f32)
            if kind == 2:
                ref[0] = out.astype(bf16)
            else:
                for at in range(0, width, 128):
                    ref[0, :, at : at + 128] = turn(out[:, at : at + 128], cosine, sine_a, sine_b).astype(bf16)

    shape.visit(rows_in, pl.program_id(1), emit)


def project(scalars, shape, pieces, parts, plan, cosine, sine_a, sine_b):
    own = next(p for p, (kind, _, _) in zip(group(shape, pieces), shape.parts) if kind == "own")[0]
    seqs, rows, width = own.shape
    local = parts[0].shape[1] // 3
    window = shape.blocks * TILE
    table = pl.BlockSpec((TILE, 128), lambda s, b, ref: (b, 0))
    whole = lambda array: pl.BlockSpec(array.shape, lambda s, b, ref: (0, 0))
    return pl.pallas_call(
        functools.partial(project_kernel, shape=shape, pieces=len(pieces), plan=plan),
        grid_spec=pltpu.PrefetchScalarGridSpec(
            num_scalar_prefetch=1,
            grid=(seqs, shape.blocks),
            in_specs=shape.specs(width) + [whole(p) for p in parts] + [table] * 3,
            out_specs=[
                pl.BlockSpec((1, TILE, local), lambda s, b, ref: (s, shape.own_block(b), 0)),
                pl.BlockSpec((1, TILE, local), lambda s, b, ref: (s, b, 0)),
                pl.BlockSpec((1, TILE, local), lambda s, b, ref: (s, b, 0)),
                pl.BlockSpec((width, 3 * local), lambda s, b, ref: (0, 0)),
            ],
        ),
        out_shape=[
            jax.ShapeDtypeStruct((seqs, rows, local), bf16),
            jax.ShapeDtypeStruct((seqs, window, local), bf16),
            jax.ShapeDtypeStruct((seqs, window, local), bf16),
            jax.ShapeDtypeStruct((width, 3 * local), bf16),
        ],
        cost_estimate=pl.CostEstimate(flops=6 << 30, transcendentals=0, bytes_accessed=16 << 20),
        name="project",
    )(scalars, *pieces, *parts, cosine, sine_a, sine_b)


def group(shape, pieces):
    out, at = [], 0
    for kind, _, _ in shape.parts:
        size = 1 if kind == "own" else 2
        out.append(pieces[at : at + size])
        at += size
    return out


def project_back_kernel(scalar_ref, *refs, shape, pieces):
    rows_in = refs[:pieces]
    dq_ref, dk_ref, dv_ref, w_ref, dout_ref, keep_ref, give_ref, grad_ref, acc_ref = refs[pieces:]
    width = dk_ref.shape[2]
    core = scalar_ref[4]
    half = w_ref.shape[0] // 2
    mine = pl.multiple_of(core * half, 16)
    other = pl.multiple_of((1 - core) * half, 16)
    start = (pl.program_id(0) == 0) & (pl.program_id(1) == 0)

    @pl.when(start)
    def _():
        acc_ref[...] = jnp.zeros_like(acc_ref)

    def emit(parts):
        full = len(parts) == 1
        grads = [(1, dk_ref[0]), (2, dv_ref[0])] + ([(0, dq_ref[0])] if full else [])
        for out_ref, at in ((keep_ref, mine), (give_ref, other)):
            total = 0.0
            for kind, grad in grads:
                total = total + across(grad, w_ref[pl.ds(at, half), kind * width : (kind + 1) * width])
            out_ref[0] = total.astype(bf16)
        for kind, grad in grads:
            cols = slice(kind * width, (kind + 1) * width)
            if full:
                acc_ref[:, cols] += contract_rows(parts[0], grad)
            else:
                acc_ref[pl.ds(mine, half), cols] += contract_rows(parts[0], grad)
                acc_ref[pl.ds(other, half), cols] += contract_rows(parts[1], grad)

    shape.visit(rows_in, pl.program_id(1), emit)

    @pl.when((pl.program_id(0) == pl.num_programs(0) - 1) & (pl.program_id(1) == pl.num_programs(1) - 1))
    def _():
        grad_ref[:, : 3 * width] = acc_ref[...].astype(bf16)
        grad_ref[:, 3 * width :] = dout_ref[...]


def project_back(scalars, shape, pieces, dq, dk, dv, weight, d_out, after):
    seqs, window, local = dk.shape
    width = weight.shape[0]
    row = pl.BlockSpec((1, TILE, local), lambda s, b, ref: (s, b, 0))
    wide = pl.BlockSpec((1, TILE, width // 2), lambda s, b, ref: (s, b, 0))
    whole = lambda array: pl.BlockSpec(array.shape, lambda s, b, ref: (0, 0))

    def kernel(scalar_ref, *refs):
        inputs = len(pieces) + 5
        project_back_kernel(
            scalar_ref, *refs[:inputs], *refs[inputs + len(after) :], shape=shape, pieces=len(pieces)
        )

    return pl.pallas_call(
        kernel,
        grid_spec=pltpu.PrefetchScalarGridSpec(
            num_scalar_prefetch=1,
            grid=(seqs, shape.blocks),
            in_specs=shape.specs(width)
            + [pl.BlockSpec((1, TILE, local), lambda s, b, ref: (s, shape.own_block(b), 0)), row, row]
            + [whole(weight), whole(d_out)]
            + [pl.BlockSpec(memory_space=pl.ANY)] * len(after),
            out_specs=[wide, wide, pl.BlockSpec((width, 4 * local), lambda s, b, ref: (0, 0))],
            scratch_shapes=[pltpu.VMEM((width, 3 * local), f32)],
        ),
        out_shape=[
            jax.ShapeDtypeStruct((seqs, window, width // 2), bf16),
            jax.ShapeDtypeStruct((seqs, window, width // 2), bf16),
            jax.ShapeDtypeStruct((width, 4 * local), bf16),
        ],
        cost_estimate=pl.CostEstimate(flops=12 << 30, transcendentals=0, bytes_accessed=32 << 20),
        name="project_back",
    )(scalars, *pieces, dq, dk, dv, weight, d_out, *after)


def head_lanes(values, head):
    lane = lax.broadcasted_iota(jnp.int32, values.shape, 1)
    inside = (lane < HD) if head == 0 else (lane >= HD)
    return jnp.where(inside, values, jnp.zeros_like(values))


def across(left, right):
    return lax.dot_general(left, right, (((1,), (1,)), ((), ())), preferred_element_type=f32)


def attend_kernel(span_ref, q_ref, k_ref, v_ref, ends_ref, o_ref, l_ref):
    seq = pl.program_id(0)
    rows = q_ref.shape[1]
    scale = HD**-0.5 * LOG2E
    for blk in range(rows // TILE):
        at = blk * TILE
        query = q_ref[0, at : at + TILE, :]
        queries = [head_lanes(query, h) for h in range(2)]
        begin, end = ends_ref[0, 0:1, at : at + TILE], ends_ref[0, 1:2, at : at + TILE]

        def step(j, carry):
            start = pl.multiple_of(j * TILE, TILE)
            keys = k_ref[0, pl.ds(start, TILE), :]
            turned = v_ref[0, pl.ds(start, TILE), :].T
            place = lax.broadcasted_iota(jnp.int32, (TILE, TILE), 0) + start
            same = (place >= begin) & (place < end)
            out = []
            for h in range(2):
                largest, total, acc = carry[h]
                scores = jnp.where(same, across(keys, queries[h]) * scale, NEG)
                bigger = jnp.maximum(largest, jnp.max(scores, 0, keepdims=True))
                probs = jnp.exp2(scores - bigger)
                shrink = jnp.exp2(largest - bigger)
                total = total * shrink + jnp.sum(probs, 0, keepdims=True)
                acc = acc * shrink + jnp.dot(
                    turned[h * HD : (h + 1) * HD], probs.astype(bf16), preferred_element_type=f32
                )
                out.append((bigger, total, acc))
            return tuple(out)

        fresh = (
            jnp.full((1, TILE), NEG, f32),
            jnp.zeros((1, TILE), f32),
            jnp.zeros((HD, TILE), f32),
        )
        low, high = span_ref[seq, 2 * blk], span_ref[seq, 2 * blk + 1]
        done = lax.fori_loop(low, high, step, (fresh, fresh))
        parts = []
        for h in range(2):
            largest, total, acc = done[h]
            parts.append(acc / total)
            l_ref[0, 0, h : h + 1, at : at + TILE] = largest + jnp.log2(total)
        o_ref[0, at : at + TILE, :] = jnp.concatenate(parts, 0).T.astype(bf16)


def attend(span, q, k, v, ends):
    seqs, rows, local = q.shape
    window = k.shape[1]
    pairs = local // 128
    whole = lambda size: pl.BlockSpec((1, size, 128), lambda s, p, span: (s, 0, p))
    return pl.pallas_call(
        attend_kernel,
        grid_spec=pltpu.PrefetchScalarGridSpec(
            num_scalar_prefetch=1,
            grid=(seqs, pairs),
            in_specs=[
                whole(rows),
                whole(window),
                whole(window),
                pl.BlockSpec((1, 2, rows), lambda s, p, span: (s, 0, 0)),
            ],
            out_specs=[
                whole(rows),
                pl.BlockSpec((1, 1, 2, rows), lambda s, p, span: (s, p, 0, 0)),
            ],
        ),
        out_shape=[
            jax.ShapeDtypeStruct((seqs, rows, local), bf16),
            jax.ShapeDtypeStruct((seqs, pairs, 2, rows), f32),
        ],
        cost_estimate=pl.CostEstimate(flops=8 << 30, transcendentals=8 << 20, bytes_accessed=8 << 20),
        name="attend",
    )(span, q, k, v, ends)


def attend_back_kernel(
    span_ref, q_ref, k_ref, v_ref, ends_ref, o_ref, l_ref, g_ref, cos_ref, sa_ref, sb_ref, *rest, first, seq
):
    dq_ref, dk_ref, dv_ref, dk_acc, dv_acc = rest[-5:]
    rows = q_ref.shape[1]
    window = k_ref.shape[1]
    factor = HD**-0.5
    scale = factor * LOG2E
    dk_acc[...] = jnp.zeros_like(dk_acc)
    dv_acc[...] = jnp.zeros_like(dv_acc)
    for blk in range(rows // TILE):
        at = blk * TILE
        query = q_ref[0, at : at + TILE, :]
        grad = g_ref[0, at : at + TILE, :]
        queries = [head_lanes(query, h) for h in range(2)]
        grads = [head_lanes(grad, h) for h in range(2)]
        product = (grad.astype(f32) * o_ref[0, at : at + TILE, :].astype(f32)).T
        deltas = [jnp.sum(product[h * HD : (h + 1) * HD], 0, keepdims=True) for h in range(2)]
        logs = [l_ref[0, 0, h : h + 1, at : at + TILE] for h in range(2)]
        begin, end = ends_ref[0, 0:1, at : at + TILE], ends_ref[0, 1:2, at : at + TILE]

        def step(j, carry):
            start = pl.multiple_of(j * TILE, TILE)
            keys = k_ref[0, pl.ds(start, TILE), :]
            vals = v_ref[0, pl.ds(start, TILE), :]
            turned = keys.T
            place = lax.broadcasted_iota(jnp.int32, (TILE, TILE), 0) + start
            same = (place >= begin) & (place < end)
            out = []
            dv = dv_acc[pl.ds(start, TILE), :]
            dk = dk_acc[pl.ds(start, TILE), :]
            for h in range(2):
                scores = jnp.where(same, across(keys, queries[h]) * scale, NEG)
                probs = jnp.exp2(scores - logs[h])
                dprobs = across(vals, grads[h])
                dscores = (probs * (dprobs - deltas[h])).astype(bf16)
                dv = dv + jnp.dot(probs.astype(bf16), grads[h], preferred_element_type=f32)
                dk = dk + jnp.dot(dscores, queries[h], preferred_element_type=f32)
                out.append(
                    carry[h]
                    + jnp.dot(turned[h * HD : (h + 1) * HD], dscores, preferred_element_type=f32)
                )
            dv_acc[pl.ds(start, TILE), :] = dv
            dk_acc[pl.ds(start, TILE), :] = dk
            return tuple(out)

        fresh = jnp.zeros((HD, TILE), f32)
        low, high = span_ref[seq, 2 * blk], span_ref[seq, 2 * blk + 1]
        done = lax.fori_loop(low, high, step, (fresh, fresh))
        dq = jnp.concatenate(done, 0).T * factor
        row = first + at
        dq_ref[0, at : at + TILE, :] = turn(
            dq, cos_ref[row : row + TILE, :], -sa_ref[row : row + TILE, :], -sb_ref[row : row + TILE, :]
        ).astype(bf16)
    for at in range(0, window, TILE):
        dk = dk_acc[at : at + TILE, :] * factor
        dk_ref[0, at : at + TILE, :] = turn(
            dk, cos_ref[at : at + TILE, :], -sa_ref[at : at + TILE, :], -sb_ref[at : at + TILE, :]
        ).astype(bf16)
        dv_ref[0, at : at + TILE, :] = dv_acc[at : at + TILE, :].astype(bf16)


def attend_back(seq, span, q, k, v, ends, out, logs, grad, cosine, sine_a, sine_b, after):
    seqs, rows, local = q.shape
    window = k.shape[1]
    pairs = local // 128
    whole = lambda size: pl.BlockSpec((1, size, 128), lambda p, span: (seq, 0, p))
    made = lambda size: pl.BlockSpec((1, size, 128), lambda p, span: (0, 0, p))
    table = pl.BlockSpec((window, 128), lambda p, span: (0, 0))
    return pl.pallas_call(
        functools.partial(attend_back_kernel, first=(window - rows) // 2, seq=seq),
        grid_spec=pltpu.PrefetchScalarGridSpec(
            num_scalar_prefetch=1,
            grid=(pairs,),
            in_specs=[
                whole(rows),
                whole(window),
                whole(window),
                pl.BlockSpec((1, 2, rows), lambda p, span: (seq, 0, 0)),
                whole(rows),
                pl.BlockSpec((1, 1, 2, rows), lambda p, span: (seq, p, 0, 0)),
                whole(rows),
                table,
                table,
                table,
            ]
            + [pl.BlockSpec(memory_space=pl.ANY)] * len(after),
            out_specs=[made(rows), made(window), made(window)],
            scratch_shapes=[pltpu.VMEM((window, 128), f32), pltpu.VMEM((window, 128), f32)],
        ),
        out_shape=[
            jax.ShapeDtypeStruct((1, rows, local), bf16),
            jax.ShapeDtypeStruct((1, window, local), bf16),
            jax.ShapeDtypeStruct((1, window, local), bf16),
        ],
        cost_estimate=pl.CostEstimate(flops=12 << 30, transcendentals=4 << 20, bytes_accessed=8 << 20),
        name="attend_back",
    )(span, q, k, v, ends, out, logs, grad, cosine, sine_a, sine_b, *after)


def norm_forward(values, gain_v, bias_v):
    average = jnp.mean(values, -1, keepdims=True)
    centred = values - average
    inv_std = lax.rsqrt(jnp.mean(centred * centred, -1, keepdims=True) + epsilon)
    unit_v = centred * inv_std
    return (unit_v * gain_v + bias_v, unit_v, inv_std)


def norm_backward(gradient, unit_v, inv_std, gain_v):
    scaled = gradient * gain_v
    dvalues = (
        scaled
        - jnp.mean(scaled, -1, keepdims=True)
        - unit_v * jnp.mean(scaled * unit_v, -1, keepdims=True)
    ) * inv_std
    return (dvalues, jnp.sum(gradient * unit_v, 0), jnp.sum(gradient, 0))


def contract_rows(left, right):
    return lax.dot_general(left, right, (((0,), (0,)), ((), ())), preferred_element_type=f32)


def contract_cols(left, right):
    return lax.dot_general(left, right, (((1,), (1,)), ((), ())), preferred_element_type=f32)


def join_tp(mine, other, me):
    return jnp.where(me == 0, jnp.concatenate([mine, other], -1), jnp.concatenate([other, mine], -1))


def reach(rows):
    left, out, far = LONGEST, [], 1
    while left > 0:
        out.append((far, min(rows, left)))
        left -= rows
        far += 1
    return out


def body(
    sizes, tokens, segments, cotangent, w_qkv, w_out, w_gate, w_up, w_down, norm_gain, norm_bias, final_gain, final_bias
):
    n_dp, n_ctx, n_tp = sizes
    me_dp, me_ctx, me_tp = lax.axis_index("dp"), lax.axis_index("ctx"), lax.axis_index("tp")
    seqs, rows, width = tokens.shape
    count = seqs * rows
    local = w_qkv.shape[2]
    hidden = w_gate.shape[1]
    own_rows = w_qkv.shape[0]
    window = rows + 2 * LONGEST
    share = width // n_tp
    scalars = jnp.stack([me_dp, me_dp ^ 1, me_dp ^ 2, me_dp ^ 3, me_tp]).astype(jnp.int32)
    direct = n_dp == 4 and own_rows % 32 == 0

    qkv_own = w_qkv.reshape(own_rows, 3 * local)
    steps = reach(rows)
    feature = lambda ref: pl.ds(pl.multiple_of(ref[4] * share, 128), share)
    copies, shapes = [], []
    for far, take in steps:
        for start in (rows - take, 0):
            src = lambda ref, start=start, take=take: (slice(None), pl.ds(start, take), feature(ref))
            copies.append((0, src, len(shapes), lambda ref: (slice(None), slice(None), slice(None))))
            shapes.append((seqs, take, share))
    gives = move(copies, [tokens], shapes, scalars, "pick_tokens")
    left, right = [], []
    if direct:
        near = sent(qkv_own, "dp", xor_perm(4, 1))
        far_w = sent(qkv_own, "dp", xor_perm(4, 2))
    for n, (far, take) in enumerate(steps):
        left.insert(0, sent(gives[2 * n], "ctx", shift_perm(n_ctx, far)))
        right.append(sent(gives[2 * n + 1], "ctx", shift_perm(n_ctx, -far)))
    docs, bit = segments, 1
    while bit < n_ctx:
        got = sent(docs, "ctx", xor_perm(n_ctx, bit))
        docs = jnp.where((me_ctx & bit) != 0, jnp.concatenate([got, docs], 1), jnp.concatenate([docs, got], 1))
        bit *= 2
    if direct:
        half = own_rows // 2
        top = sent(near[:half], "dp", xor_perm(4, 2))
        low = sent(far_w[half:], "dp", xor_perm(4, 1))
        parts = [qkv_own, near, far_w, top, low]
        plan = [(0, own_rows, 0), (1, own_rows, 0), (2, own_rows, 0), (3, own_rows, 0), (3, own_rows, half)]
    else:
        parts, plan = [gather_rows(qkv_own, me_dp, n_dp)], [(0, 0, 0)]

    lines = jnp.stack([norm_gain, norm_bias, final_gain, final_bias], 1)
    lines = jnp.pad(lines, ((0, 0), (0, 124)))
    cuts = [(0, local), (local, local + 128)]
    for n in range(3):
        cuts.append((cuts[-1][1], cuts[-1][1] + hidden))
    rest_cols = cuts[-1][1]
    owned = [w_out, lines, w_gate, w_up, w_down]
    everything = lambda ref: (slice(None), slice(None))
    if direct:
        (rest,) = move(
            [(n, everything, 0, all_rows(*cut)) for n, cut in enumerate(cuts)],
            owned,
            [(own_rows, rest_cols)],
            scalars,
            "pack_weights",
        )
        rest, _ = lax.optimization_barrier((rest, (top, low)))
        got = fetch_rows(rest)
        copies = []
        for n, cut in enumerate(cuts):
            cols = slice(*cut)
            target = lambda k, offset, size: rows_at(k, (own_rows, offset), size)
            copies.append((n, everything, n, target(0, 0, own_rows)))
            for g, (k, offset, size) in enumerate(((1, 0, own_rows), (2, 0, own_rows), (3, 0, half), (3, half, half))):
                copies.append((len(owned) + g, all_rows(*cut), n, target(k, offset, size)))
        out_w, lines, gate_w, up_w, down_w = move(
            copies, owned + list(got), [(width, hi - lo) for lo, hi in cuts], scalars, "place_weights"
        )
    else:
        out_w, lines, gate_w, up_w, down_w = [gather_rows(w, me_dp, n_dp) for w in owned]
    params = lines[:, :4].astype(f32).T
    gain_one, bias_one, gain_two, bias_two = params[0], params[1], params[2], params[3]

    quarter = HD // 2
    places = (me_ctx * rows - LONGEST + jnp.arange(window)).astype(f32)
    inverse = rotary_base ** (-(jnp.arange(quarter).astype(f32) * 2.0 / HD))
    angles = places[:, None] * jnp.concatenate([inverse] * 4)[None, :]
    lead = (jnp.arange(128) % HD) < quarter
    cos_t, sine = jnp.cos(angles), jnp.sin(angles)
    sin_a = jnp.where(lead[None, :], -sine, 0.0)
    sin_b = jnp.where(lead[None, :], 0.0, sine)

    offset = LONGEST - me_ctx * rows
    below = jnp.sum(docs[:, None, :] < jnp.arange(9)[None, :, None], -1).astype(jnp.int32)
    is_doc = segments[:, None, :] == jnp.arange(8)[None, :, None]
    begin = jnp.sum(jnp.where(is_doc, below[:, :8, None], 0), 1) + offset
    end = jnp.sum(jnp.where(is_doc, below[:, 1:, None], 0), 1) + offset
    ends = jnp.stack([begin, end], 1)
    spans = []
    for at in range(0, rows, TILE):
        spans += [begin[:, at] // TILE, (end[:, at + TILE - 1] + TILE - 1) // TILE]
    span = jnp.stack(spans, 1)

    shape = Window(seqs, rows, [p.shape[1] for p in left], [p.shape[1] for p in right])
    pieces = []
    for piece in left:
        pieces += [piece, sent(piece, "tp", xor_perm(n_tp, 1))]
    pieces.append(tokens)
    for piece in right:
        pieces += [piece, sent(piece, "tp", xor_perm(n_tp, 1))]
    q, k, v, qkv_w = project(scalars, shape, pieces, parts, plan, cos_t, sin_a, sin_b)
    mixture, logs = attend(span, q, k, v, ends)

    flat = tokens.reshape(count, width)
    mixture_flat = mixture.reshape(count, local)
    attended = add_over_tp(contract_cols(mixture_flat, out_w), n_tp)
    normed, unit_one, inv_one = norm_forward(flat.astype(f32) + attended, gain_one, bias_one)
    normed_low = normed.astype(bf16)
    gate_pre = jnp.dot(normed_low, gate_w, preferred_element_type=f32)
    up_pre = jnp.dot(normed_low, up_w, preferred_element_type=f32)
    sigmoid_g = jax.nn.sigmoid(gate_pre)
    activated = gate_pre * sigmoid_g
    hidden_low = (activated * up_pre).astype(bf16)
    branch = add_over_tp(contract_cols(hidden_low, down_w), n_tp)
    final_out, unit_two, inv_two = norm_forward(normed + branch, gain_two, bias_two)
    output = final_out.astype(bf16).reshape(seqs, rows, width)

    grad_out = cotangent.reshape(count, width).astype(f32)
    dsum, dgain_two, dbias_two = norm_backward(grad_out, unit_two, inv_two, gain_two)
    dbranch = dsum.astype(bf16)
    mine = (me_dp, me_ctx)
    r_down = Reduction(contract_rows(dbranch, hidden_low).astype(bf16), sizes, mine, scalars, "down").first()
    dhidden = jnp.dot(dbranch, down_w, preferred_element_type=f32)
    dgate = (dhidden * up_pre * sigmoid_g * (1.0 + gate_pre * (1.0 - sigmoid_g))).astype(bf16)
    dup = (dhidden * activated).astype(bf16)
    dnormed_part = contract_cols(dgate, gate_w) + contract_cols(dup, up_w)
    dnormed = dsum + add_over_tp(dnormed_part, n_tp)
    r_gate = Reduction(contract_rows(normed_low, dgate).astype(bf16), sizes, mine, scalars, "gate").first()
    r_up = Reduction(contract_rows(normed_low, dup).astype(bf16), sizes, mine, scalars, "up").first()
    dresid, dgain_one, dbias_one = norm_backward(dnormed, unit_one, inv_one, gain_one)
    dattended = dresid.astype(bf16)
    d_out = contract_rows(dattended, mixture_flat).astype(bf16)
    dmixture = jnp.dot(dattended, out_w, preferred_element_type=f32).astype(bf16).reshape(seqs, rows, local)

    token = lambda *steps: [r.token for r in steps if r.direct]
    r_down.second()
    small = total_small(jnp.stack([dgain_one, dbias_one, dgain_two, dbias_two]), me_dp, sizes)
    backs = []
    for seq in range(seqs):
        backs.append(
            attend_back(
                seq, span, q, k, v, ends, mixture, logs, dmixture, cos_t, sin_a, sin_b, token(r_down, r_gate, r_up)
            )
        )
        done = backs[-1][0]
        if seq == 0:
            r_down.inward(done)
            r_gate.second(done)
            r_up.second(done)
    r_down.across(done)
    r_gate.inward(done)
    r_up.inward(done)
    dq, dk, dv = [jnp.concatenate(kind, 0) for kind in zip(*backs)]
    keep, give, d_last = project_back(
        scalars, shape, pieces, dq, dk, dv, qkv_w, d_out, token(r_down, r_gate, r_up)
    )
    r_last = Reduction(d_last, sizes, mine, scalars, "last").first()
    r_down.outward(d_last)
    r_gate.across(d_last)
    r_up.across(d_last)

    dx_half = keep.astype(f32) + sent(give, "tp", xor_perm(n_tp, 1)).astype(f32)
    total = dx_half[:, LONGEST : LONGEST + rows]
    at = LONGEST
    for far, take in steps:
        to_left = dx_half[:, at - take : at].astype(bf16)
        to_right = dx_half[:, window - at : window - at + take].astype(bf16)
        from_right = sent(to_left, "ctx", shift_perm(n_ctx, -far)).astype(f32)
        from_left = sent(to_right, "ctx", shift_perm(n_ctx, far)).astype(f32)
        pad = rows - take
        total = total + jnp.pad(from_right, ((0, 0), (pad, 0), (0, 0))) + jnp.pad(from_left, ((0, 0), (0, pad), (0, 0)))
        at -= take
    r_last.second()
    r_gate.outward()
    r_up.outward()
    r_last.inward().across().outward()
    half_in = total.astype(bf16)
    dinput = join_tp(half_in, sent(half_in, "tp", xor_perm(n_tp, 1)), me_tp).reshape(count, width)
    d_tokens = (dresid + dinput.astype(f32)).astype(bf16).reshape(seqs, rows, width)

    g_last = r_last.result()
    g_qkv = g_last[:, : 3 * local].reshape(own_rows, 3, local)
    g_out = g_last[:, 3 * local :]
    return (
        output,
        d_tokens,
        g_qkv,
        g_out,
        r_gate.result(),
        r_up.result(),
        r_down.result(),
        small[0],
        small[1],
        small[2],
        small[3],
    )


def solution(mesh):
    sizes = (mesh.shape["dp"], mesh.shape["ctx"], mesh.shape["tp"])
    wide, flat, kinds, square, line = (
        P("dp", "ctx", None),
        P("dp", "ctx"),
        P("dp", None, "tp"),
        P("dp", "tp"),
        P("dp"),
    )
    return jax.shard_map(
        functools.partial(body, sizes),
        mesh=mesh,
        in_specs=(wide, flat, wide, kinds) + (square,) * 4 + (line,) * 4,
        out_specs=(wide, wide, kinds) + (square,) * 4 + (line,) * 4,
        check_vma=False,
    )
```

```python
import functools

import jax
import jax.numpy as jnp
from jax import lax
from jax.experimental import pallas as pl
from jax.experimental.pallas import tpu as pltpu
from jax.sharding import PartitionSpec as P

HD = 64
LONGEST = 768
TILE = 256

epsilon = 1e-12
rotary_base = 1000.0
NEG = -1e30
LOG2E = 1.4426950408889634


bf16 = jnp.bfloat16
f32 = jnp.float32


def xor_perm(count, bit):
    return [(i, i ^ bit) for i in range(count)]


def shift_perm(count, by):
    return [(i, i + by) for i in range(count) if 0 <= i + by < count]


def sent(values, axis, perm):
    return lax.ppermute(values, axis, perm)


def move(copies, sources, shapes, scalars, name):
    count = len(sources)

    def kernel(scalar_ref, *refs):
        given, made = refs[:count], refs[count : count + len(shapes)]
        held, sems_in, sems_out = refs[count + len(shapes) : -2], refs[-2], refs[-1]
        inward = []
        for n, (src, src_at, _, _, _) in enumerate(copies):
            inward.append(pltpu.make_async_copy(given[src].at[src_at(scalar_ref)], held[n], sems_in.at[n]))
            inward[-1].start()
        outward = []
        for n, (_, _, dst, dst_at, _) in enumerate(copies):
            inward[n].wait()
            outward.append(pltpu.make_async_copy(held[n], made[dst].at[dst_at(scalar_ref)], sems_out.at[n]))
            outward[-1].start()
        for copy in outward:
            copy.wait()

    anywhere = pl.BlockSpec(memory_space=pl.ANY)
    return pl.pallas_call(
        kernel,
        grid_spec=pltpu.PrefetchScalarGridSpec(
            num_scalar_prefetch=1,
            grid=(),
            in_specs=[anywhere] * count,
            out_specs=[anywhere] * len(shapes),
            scratch_shapes=[pltpu.VMEM(copy[4], bf16) for copy in copies]
            + [pltpu.SemaphoreType.DMA((len(copies),))] * 2,
        ),
        out_shape=[jax.ShapeDtypeStruct(shape, bf16) for shape in shapes],
        name=name,
    )(scalars, *sources)


def rows_at(index, start, size):
    return lambda ref: (pl.ds(pl.multiple_of(ref[index] * start[0] + start[1], 16), size), slice(None))


def all_rows(*cols):
    cut = slice(*cols) if cols else slice(None)
    return lambda ref: (slice(None), cut)


def fetch_rows(own, after=None):
    half = own.shape[0] // 2
    near = sent(own, "dp", xor_perm(4, 1))
    far = sent(own, "dp", xor_perm(4, 2))
    top = sent(near[:half], "dp", xor_perm(4, 2))
    low = sent(far[half:], "dp", xor_perm(4, 1))
    return near, far, top, low


def gather_rows(own, me, count):
    bit = 1
    while bit < count:
        got = sent(own, "dp", xor_perm(count, bit))
        own = jnp.where((me & bit) != 0, jnp.concatenate([got, own], 0), jnp.concatenate([own, got], 0))
        bit *= 2
    return own


def scatter_rows(grad, me, count):
    bit, grad = count // 2, grad.astype(f32)
    while bit >= 1:
        half = grad.shape[0] // 2
        side = jnp.where((me & bit) != 0, 1, 0)
        give = lax.dynamic_slice_in_dim(grad, (1 - side) * half, half, 0).astype(bf16)
        grad = lax.dynamic_slice_in_dim(grad, side * half, half, 0)
        grad = grad + sent(give, "dp", xor_perm(count, bit)).astype(f32)
        bit //= 2
    return grad.astype(bf16)


def add_kernel(scalar_ref, *refs, rows, terms, stack):
    made = refs[-1:] if stack else refs[-len(terms) :]
    at = 0
    for n, count in enumerate(terms):
        total = refs[at][...].astype(f32)
        for k in range(1, count):
            total = total + refs[at + k][...].astype(f32)
        if stack:
            made[0][n * rows : (n + 1) * rows] = total.astype(bf16)
        else:
            made[n][...] = total.astype(bf16)
        at += count


def add_blocks(scalars, sums, rows, cols, after, name, stack=False):
    outs, height = (1, rows * len(sums)) if stack else (len(sums), rows)
    specs, values, terms = [], [], []
    step = cols
    for parts in sums:
        terms.append(len(parts))
        for array, index in parts:
            if callable(index):
                at = lambda c, ref, index=index: (index(ref), c)
            else:
                at = lambda c, ref, index=index: (index, c)
            specs.append(pl.BlockSpec((rows, step), at))
            values.append(array)
    anywhere = pl.BlockSpec(memory_space=pl.ANY)
    return pl.pallas_call(
        functools.partial(add_kernel, rows=rows, terms=terms, stack=stack),
        grid_spec=pltpu.PrefetchScalarGridSpec(
            num_scalar_prefetch=1,
            grid=(cols // step,),
            in_specs=specs + [anywhere] * len(after),
            out_specs=[pl.BlockSpec((height, step), lambda c, ref: (0, c))] * outs,
        ),
        out_shape=[jax.ShapeDtypeStruct((height, cols), bf16)] * outs,
        name=name,
    )(scalars, *values, *after)


class Reduction:
    def __init__(self, grad, sizes, mine, scalars, name):
        self.grad, self.name, self.scalars = grad, name, scalars
        self.n_dp, self.n_ctx, _ = sizes
        self.me_dp, self.me_ctx = mine
        self.rows, self.cols = grad.shape[0] // self.n_dp, grad.shape[1]
        self.half = self.rows // 2
        self.direct = self.n_dp == 4 and self.half % 16 == 0

    def first(self):
        if not self.direct:
            self.part = scatter_rows(self.grad, self.me_dp, self.n_dp)
            return self
        rows, half = self.rows, self.half
        cut = lambda k, offset: rows_at(k, (rows, offset), half)
        at = lambda start: lambda ref: (pl.ds(start, half), slice(None))
        x_give, y_give = move(
            [
                (0, cut(3, 0), 0, at(0), (half, self.cols)),
                (0, cut(3, half), 1, at(0), (half, self.cols)),
                (0, cut(1, 0), 0, at(half), (half, self.cols)),
                (0, cut(2, half), 1, at(half), (half, self.cols)),
            ],
            [self.grad],
            [(rows, self.cols)] * 2,
            self.scalars,
            "pick_" + self.name,
        )
        self.token = x_give
        self.x_got = sent(x_give, "dp", xor_perm(4, 1))
        self.y_got = sent(y_give, "dp", xor_perm(4, 2))
        return self

    def second(self, *after):
        if not self.direct:
            return self
        x_next, y_next = add_blocks(
            self.scalars,
            [
                [(self.grad, lambda ref: ref[1] * 2 + 1), (self.y_got, 0)],
                [(self.grad, lambda ref: ref[2] * 2), (self.x_got, 0)],
            ],
            self.half,
            self.cols,
            after,
            "add_second_" + self.name,
        )
        self.token = x_next
        self.x_last = sent(x_next, "dp", xor_perm(4, 1))
        self.y_last = sent(y_next, "dp", xor_perm(4, 2))
        return self

    def inward(self, *after):
        if self.direct:
            (self.part,) = add_blocks(
                self.scalars,
                [
                    [(self.grad, lambda ref: ref[0] * 2), (self.x_got, 1), (self.y_last, 0)],
                    [(self.grad, lambda ref: ref[0] * 2 + 1), (self.y_got, 1), (self.x_last, 0)],
                ],
                self.half,
                self.cols,
                after,
                "add_inward_" + self.name,
                stack=True,
            )
        if self.n_ctx == 4:
            self.got = sent(self.part, "ctx", [(0, 1), (3, 2)])
        self.token = self.part
        return self

    def plus(self, name, after):
        if self.rows % 16 == 0:
            (self.part,) = add_blocks(
                self.scalars, [[(self.part, 0), (self.got, 0)]], self.rows, self.cols, after, name + self.name
            )
        else:
            self.part = (self.part.astype(f32) + self.got.astype(f32)).astype(bf16)
        self.token = self.part

    def across(self, *after):
        if self.n_ctx == 4:
            self.plus("add_across_", after)
            self.got = sent(self.part, "ctx", [(1, 2), (2, 1)])
        return self

    def outward(self, *after):
        if self.n_ctx == 4:
            self.plus("add_outward_", after)
            self.got = sent(self.part, "ctx", [(1, 0), (2, 3)])
        return self

    def result(self):
        if self.n_ctx == 4:
            edge = (self.me_ctx == 0) | (self.me_ctx == 3)
            return jnp.where(edge, self.got, self.part).astype(f32)
        part, bit = self.part, 1
        while bit < self.n_ctx:
            got = sent(part, "ctx", xor_perm(self.n_ctx, bit))
            part = (part.astype(f32) + got.astype(f32)).astype(bf16)
            bit *= 2
        return part.astype(f32)


def total_small(part, me, sizes):
    n_dp, n_ctx, _ = sizes
    bit = n_dp // 2
    while bit >= 1:
        half = part.shape[1] // 2
        side = jnp.where((me & bit) != 0, 1, 0)
        give = lax.dynamic_slice_in_dim(part, (1 - side) * half, half, 1)
        part = lax.dynamic_slice_in_dim(part, side * half, half, 1) + sent(give, "dp", xor_perm(n_dp, bit))
        bit //= 2
    bit = 1
    while bit < n_ctx:
        part = part + sent(part, "ctx", xor_perm(n_ctx, bit))
        bit *= 2
    return part


def add_over_tp(part, count):
    low = part.astype(bf16)
    bit = 1
    total = low
    while bit < count:
        got = lax.ppermute(total, "tp", xor_perm(count, bit))
        total = total.astype(f32) + got.astype(f32)
        bit *= 2
    return total.astype(f32)


def turn(values, cosine, sine_a, sine_b):
    width = values.shape[-1]
    ahead = pltpu.roll(values, width - HD // 2, 1)
    behind = pltpu.roll(values, HD // 2, 1)
    return values * cosine + ahead * sine_a + behind * sine_b


class Window:
    def __init__(self, seqs, rows, pieces_left, pieces_right):
        self.parts = []
        at = 0
        for kind, sizes in (("left", pieces_left), ("own", [rows]), ("right", pieces_right)):
            for n, size in enumerate(sizes):
                self.parts.append((kind, at, at + size // TILE))
                at += size // TILE
        self.blocks = at
        self.first, self.last = next((lo, hi) for kind, lo, hi in self.parts if kind == "own")

    def own_block(self, b):
        return jnp.clip(b - self.first, 0, self.last - self.first - 1)

    def specs(self, width):
        out = []
        for kind, lo, hi in self.parts:
            at = lambda s, b, *ref, lo=lo, hi=hi: (s, jnp.clip(b - lo, 0, hi - lo - 1), 0)
            if kind == "own":
                out.append(pl.BlockSpec((1, TILE, width), at))
            else:
                out += [pl.BlockSpec((1, TILE, width // 2), at)] * 2
        return out

    def visit(self, refs, block, emit):
        at = 0
        for kind, lo, hi in self.parts:
            mine = refs[at : at + (1 if kind == "own" else 2)]
            at += len(mine)

            @pl.when((block >= lo) & (block < hi))
            def _():
                emit([ref[0] for ref in mine])


def project_kernel(scalar_ref, *refs, shape, pieces, plan):
    rows_in = refs[:pieces]
    weights = refs[pieces : pieces + len(plan)]
    cos_ref, sa_ref, sb_ref, q_ref, k_ref, v_ref, w_ref = refs[pieces + len(plan) :]
    width = k_ref.shape[2]
    core = scalar_ref[4]

    @pl.when((pl.program_id(0) == 0) & (pl.program_id(1) == 0))
    def _():
        for ref, (index, size, offset) in zip(weights, plan):
            rows = ref.shape[0]
            w_ref[pl.ds(pl.multiple_of(scalar_ref[index] * size + offset, 16), rows), :] = ref[...]

    cosine, sine_a, sine_b = cos_ref[...], sa_ref[...], sb_ref[...]

    def emit(parts):
        full = len(parts) == 1
        half = w_ref.shape[0] // 2
        for kind, ref in ((0, q_ref), (1, k_ref), (2, v_ref)):
            if kind == 0 and not full:
                continue
            cols = slice(kind * width, (kind + 1) * width)
            if full:
                out = jnp.dot(parts[0], w_ref[:, cols], preferred_element_type=f32)
            else:
                mine = pl.multiple_of(core * half, 16)
                other = pl.multiple_of((1 - core) * half, 16)
                out = jnp.dot(parts[0], w_ref[pl.ds(mine, half), cols], preferred_element_type=f32)
                out = out + jnp.dot(parts[1], w_ref[pl.ds(other, half), cols], preferred_element_type=f32)
            if kind == 2:
                ref[0] = out.astype(bf16)
            else:
                for at in range(0, width, 128):
                    ref[0, :, at : at + 128] = turn(out[:, at : at + 128], cosine, sine_a, sine_b).astype(bf16)

    shape.visit(rows_in, pl.program_id(1), emit)


def project(scalars, shape, pieces, parts, plan, cosine, sine_a, sine_b):
    own = next(p for p, (kind, _, _) in zip(group(shape, pieces), shape.parts) if kind == "own")[0]
    seqs, rows, width = own.shape
    local = parts[0].shape[1] // 3
    window = shape.blocks * TILE
    table = pl.BlockSpec((TILE, 128), lambda s, b, ref: (b, 0))
    whole = lambda array: pl.BlockSpec(array.shape, lambda s, b, ref: (0, 0))
    return pl.pallas_call(
        functools.partial(project_kernel, shape=shape, pieces=len(pieces), plan=plan),
        grid_spec=pltpu.PrefetchScalarGridSpec(
            num_scalar_prefetch=1,
            grid=(seqs, shape.blocks),
            in_specs=shape.specs(width) + [whole(p) for p in parts] + [table] * 3,
            out_specs=[
                pl.BlockSpec((1, TILE, local), lambda s, b, ref: (s, shape.own_block(b), 0)),
                pl.BlockSpec((1, TILE, local), lambda s, b, ref: (s, b, 0)),
                pl.BlockSpec((1, TILE, local), lambda s, b, ref: (s, b, 0)),
                pl.BlockSpec((width, 3 * local), lambda s, b, ref: (0, 0)),
            ],
        ),
        out_shape=[
            jax.ShapeDtypeStruct((seqs, rows, local), bf16),
            jax.ShapeDtypeStruct((seqs, window, local), bf16),
            jax.ShapeDtypeStruct((seqs, window, local), bf16),
            jax.ShapeDtypeStruct((width, 3 * local), bf16),
        ],
        cost_estimate=pl.CostEstimate(flops=6 << 30, transcendentals=0, bytes_accessed=16 << 20),
        name="project",
    )(scalars, *pieces, *parts, cosine, sine_a, sine_b)


def group(shape, pieces):
    out, at = [], 0
    for kind, _, _ in shape.parts:
        size = 1 if kind == "own" else 2
        out.append(pieces[at : at + size])
        at += size
    return out


def project_back_kernel(scalar_ref, *refs, shape, pieces):
    rows_in = refs[:pieces]
    dq_ref, dk_ref, dv_ref, w_ref, dout_ref, keep_ref, give_ref, grad_ref, acc_ref = refs[pieces:]
    width = dk_ref.shape[2]
    core = scalar_ref[4]
    half = w_ref.shape[0] // 2
    mine = pl.multiple_of(core * half, 16)
    other = pl.multiple_of((1 - core) * half, 16)
    start = (pl.program_id(0) == 0) & (pl.program_id(1) == 0)

    @pl.when(start)
    def _():
        acc_ref[...] = jnp.zeros_like(acc_ref)

    def emit(parts):
        full = len(parts) == 1
        grads = [(1, dk_ref[0]), (2, dv_ref[0])] + ([(0, dq_ref[0])] if full else [])
        for out_ref, at in ((keep_ref, mine), (give_ref, other)):
            total = 0.0
            for kind, grad in grads:
                total = total + across(grad, w_ref[pl.ds(at, half), kind * width : (kind + 1) * width])
            out_ref[0] = total.astype(bf16)
        for kind, grad in grads:
            cols = slice(kind * width, (kind + 1) * width)
            if full:
                acc_ref[:, cols] += contract_rows(parts[0], grad)
            else:
                acc_ref[pl.ds(mine, half), cols] += contract_rows(parts[0], grad)
                acc_ref[pl.ds(other, half), cols] += contract_rows(parts[1], grad)

    shape.visit(rows_in, pl.program_id(1), emit)

    @pl.when((pl.program_id(0) == pl.num_programs(0) - 1) & (pl.program_id(1) == pl.num_programs(1) - 1))
    def _():
        grad_ref[:, : 3 * width] = acc_ref[...].astype(bf16)
        grad_ref[:, 3 * width :] = dout_ref[...]


def project_back(scalars, shape, pieces, dq, dk, dv, weight, d_out, after):
    seqs, window, local = dk.shape
    width = weight.shape[0]
    row = pl.BlockSpec((1, TILE, local), lambda s, b, ref: (s, b, 0))
    wide = pl.BlockSpec((1, TILE, width // 2), lambda s, b, ref: (s, b, 0))
    whole = lambda array: pl.BlockSpec(array.shape, lambda s, b, ref: (0, 0))

    def kernel(scalar_ref, *refs):
        inputs = len(pieces) + 5
        project_back_kernel(
            scalar_ref, *refs[:inputs], *refs[inputs + len(after) :], shape=shape, pieces=len(pieces)
        )

    return pl.pallas_call(
        kernel,
        grid_spec=pltpu.PrefetchScalarGridSpec(
            num_scalar_prefetch=1,
            grid=(seqs, shape.blocks),
            in_specs=shape.specs(width)
            + [pl.BlockSpec((1, TILE, local), lambda s, b, ref: (s, shape.own_block(b), 0)), row, row]
            + [whole(weight), whole(d_out)]
            + [pl.BlockSpec(memory_space=pl.ANY)] * len(after),
            out_specs=[wide, wide, pl.BlockSpec((width, 4 * local), lambda s, b, ref: (0, 0))],
            scratch_shapes=[pltpu.VMEM((width, 3 * local), f32)],
        ),
        out_shape=[
            jax.ShapeDtypeStruct((seqs, window, width // 2), bf16),
            jax.ShapeDtypeStruct((seqs, window, width // 2), bf16),
            jax.ShapeDtypeStruct((width, 4 * local), bf16),
        ],
        cost_estimate=pl.CostEstimate(flops=12 << 30, transcendentals=0, bytes_accessed=32 << 20),
        name="project_back",
    )(scalars, *pieces, dq, dk, dv, weight, d_out, *after)


def head_lanes(values, head):
    lane = lax.broadcasted_iota(jnp.int32, values.shape, 1)
    inside = (lane < HD) if head == 0 else (lane >= HD)
    return jnp.where(inside, values, jnp.zeros_like(values))


def across(left, right):
    return lax.dot_general(left, right, (((1,), (1,)), ((), ())), preferred_element_type=f32)


def attend_kernel(span_ref, q_ref, k_ref, v_ref, ends_ref, o_ref, l_ref):
    seq = pl.program_id(0)
    rows = q_ref.shape[1]
    scale = HD**-0.5 * LOG2E
    for blk in range(rows // TILE):
        at = blk * TILE
        query = q_ref[0, at : at + TILE, :]
        queries = [head_lanes(query, h) for h in range(2)]
        begin, end = ends_ref[0, 0:1, at : at + TILE], ends_ref[0, 1:2, at : at + TILE]

        def step(j, carry):
            start = pl.multiple_of(j * TILE, TILE)
            keys = k_ref[0, pl.ds(start, TILE), :]
            turned = v_ref[0, pl.ds(start, TILE), :].T
            place = lax.broadcasted_iota(jnp.int32, (TILE, TILE), 0) + start
            same = (place >= begin) & (place < end)
            out = []
            for h in range(2):
                largest, total, acc = carry[h]
                scores = jnp.where(same, across(keys, queries[h]) * scale, NEG)
                bigger = jnp.maximum(largest, jnp.max(scores, 0, keepdims=True))
                probs = jnp.exp2(scores - bigger)
                shrink = jnp.exp2(largest - bigger)
                total = total * shrink + jnp.sum(probs, 0, keepdims=True)
                acc = acc * shrink + jnp.dot(
                    turned[h * HD : (h + 1) * HD], probs.astype(bf16), preferred_element_type=f32
                )
                out.append((bigger, total, acc))
            return tuple(out)

        fresh = (
            jnp.full((1, TILE), NEG, f32),
            jnp.zeros((1, TILE), f32),
            jnp.zeros((HD, TILE), f32),
        )
        low, high = span_ref[seq, 2 * blk], span_ref[seq, 2 * blk + 1]
        done = lax.fori_loop(low, high, step, (fresh, fresh))
        parts = []
        for h in range(2):
            largest, total, acc = done[h]
            parts.append(acc / total)
            l_ref[0, 0, h : h + 1, at : at + TILE] = largest + jnp.log2(total)
        o_ref[0, at : at + TILE, :] = jnp.concatenate(parts, 0).T.astype(bf16)


def attend(span, q, k, v, ends):
    seqs, rows, local = q.shape
    window = k.shape[1]
    pairs = local // 128
    whole = lambda size: pl.BlockSpec((1, size, 128), lambda s, p, span: (s, 0, p))
    return pl.pallas_call(
        attend_kernel,
        grid_spec=pltpu.PrefetchScalarGridSpec(
            num_scalar_prefetch=1,
            grid=(seqs, pairs),
            in_specs=[
                whole(rows),
                whole(window),
                whole(window),
                pl.BlockSpec((1, 2, rows), lambda s, p, span: (s, 0, 0)),
            ],
            out_specs=[
                whole(rows),
                pl.BlockSpec((1, 1, 2, rows), lambda s, p, span: (s, p, 0, 0)),
            ],
        ),
        out_shape=[
            jax.ShapeDtypeStruct((seqs, rows, local), bf16),
            jax.ShapeDtypeStruct((seqs, pairs, 2, rows), f32),
        ],
        cost_estimate=pl.CostEstimate(flops=8 << 30, transcendentals=8 << 20, bytes_accessed=8 << 20),
        name="attend",
    )(span, q, k, v, ends)


def attend_back_kernel(
    span_ref, q_ref, k_ref, v_ref, ends_ref, o_ref, l_ref, g_ref, cos_ref, sa_ref, sb_ref, *rest, first, seq
):
    dq_ref, dk_ref, dv_ref, dk_acc, dv_acc = rest[-5:]
    rows = q_ref.shape[1]
    window = k_ref.shape[1]
    factor = HD**-0.5
    scale = factor * LOG2E
    dk_acc[...] = jnp.zeros_like(dk_acc)
    dv_acc[...] = jnp.zeros_like(dv_acc)
    for blk in range(rows // TILE):
        at = blk * TILE
        query = q_ref[0, at : at + TILE, :]
        grad = g_ref[0, at : at + TILE, :]
        queries = [head_lanes(query, h) for h in range(2)]
        grads = [head_lanes(grad, h) for h in range(2)]
        product = (grad.astype(f32) * o_ref[0, at : at + TILE, :].astype(f32)).T
        deltas = [jnp.sum(product[h * HD : (h + 1) * HD], 0, keepdims=True) for h in range(2)]
        logs = [l_ref[0, 0, h : h + 1, at : at + TILE] for h in range(2)]
        begin, end = ends_ref[0, 0:1, at : at + TILE], ends_ref[0, 1:2, at : at + TILE]

        def step(j, carry):
            start = pl.multiple_of(j * TILE, TILE)
            keys = k_ref[0, pl.ds(start, TILE), :]
            vals = v_ref[0, pl.ds(start, TILE), :]
            turned = keys.T
            place = lax.broadcasted_iota(jnp.int32, (TILE, TILE), 0) + start
            same = (place >= begin) & (place < end)
            out = []
            dv = dv_acc[pl.ds(start, TILE), :]
            dk = dk_acc[pl.ds(start, TILE), :]
            for h in range(2):
                scores = jnp.where(same, across(keys, queries[h]) * scale, NEG)
                probs = jnp.exp2(scores - logs[h])
                dprobs = across(vals, grads[h])
                dscores = (probs * (dprobs - deltas[h])).astype(bf16)
                dv = dv + jnp.dot(probs.astype(bf16), grads[h], preferred_element_type=f32)
                dk = dk + jnp.dot(dscores, queries[h], preferred_element_type=f32)
                out.append(
                    carry[h]
                    + jnp.dot(turned[h * HD : (h + 1) * HD], dscores, preferred_element_type=f32)
                )
            dv_acc[pl.ds(start, TILE), :] = dv
            dk_acc[pl.ds(start, TILE), :] = dk
            return tuple(out)

        fresh = jnp.zeros((HD, TILE), f32)
        low, high = span_ref[seq, 2 * blk], span_ref[seq, 2 * blk + 1]
        done = lax.fori_loop(low, high, step, (fresh, fresh))
        dq = jnp.concatenate(done, 0).T * factor
        row = first + at
        dq_ref[0, at : at + TILE, :] = turn(
            dq, cos_ref[row : row + TILE, :], -sa_ref[row : row + TILE, :], -sb_ref[row : row + TILE, :]
        ).astype(bf16)
    for at in range(0, window, TILE):
        dk = dk_acc[at : at + TILE, :] * factor
        dk_ref[0, at : at + TILE, :] = turn(
            dk, cos_ref[at : at + TILE, :], -sa_ref[at : at + TILE, :], -sb_ref[at : at + TILE, :]
        ).astype(bf16)
        dv_ref[0, at : at + TILE, :] = dv_acc[at : at + TILE, :].astype(bf16)


def attend_back(seq, span, q, k, v, ends, out, logs, grad, cosine, sine_a, sine_b, after):
    seqs, rows, local = q.shape
    window = k.shape[1]
    pairs = local // 128
    whole = lambda size: pl.BlockSpec((1, size, 128), lambda p, span: (seq, 0, p))
    made = lambda size: pl.BlockSpec((1, size, 128), lambda p, span: (0, 0, p))
    table = pl.BlockSpec((window, 128), lambda p, span: (0, 0))
    return pl.pallas_call(
        functools.partial(attend_back_kernel, first=(window - rows) // 2, seq=seq),
        grid_spec=pltpu.PrefetchScalarGridSpec(
            num_scalar_prefetch=1,
            grid=(pairs,),
            in_specs=[
                whole(rows),
                whole(window),
                whole(window),
                pl.BlockSpec((1, 2, rows), lambda p, span: (seq, 0, 0)),
                whole(rows),
                pl.BlockSpec((1, 1, 2, rows), lambda p, span: (seq, p, 0, 0)),
                whole(rows),
                table,
                table,
                table,
            ]
            + [pl.BlockSpec(memory_space=pl.ANY)] * len(after),
            out_specs=[made(rows), made(window), made(window)],
            scratch_shapes=[pltpu.VMEM((window, 128), f32), pltpu.VMEM((window, 128), f32)],
        ),
        out_shape=[
            jax.ShapeDtypeStruct((1, rows, local), bf16),
            jax.ShapeDtypeStruct((1, window, local), bf16),
            jax.ShapeDtypeStruct((1, window, local), bf16),
        ],
        cost_estimate=pl.CostEstimate(flops=12 << 30, transcendentals=4 << 20, bytes_accessed=8 << 20),
        name="attend_back",
    )(span, q, k, v, ends, out, logs, grad, cosine, sine_a, sine_b, *after)


def norm_forward(values, gain_v, bias_v):
    average = jnp.mean(values, -1, keepdims=True)
    centred = values - average
    inv_std = lax.rsqrt(jnp.mean(centred * centred, -1, keepdims=True) + epsilon)
    unit_v = centred * inv_std
    return (unit_v * gain_v + bias_v, unit_v, inv_std)


def norm_backward(gradient, unit_v, inv_std, gain_v):
    scaled = gradient * gain_v
    dvalues = (
        scaled
        - jnp.mean(scaled, -1, keepdims=True)
        - unit_v * jnp.mean(scaled * unit_v, -1, keepdims=True)
    ) * inv_std
    return (dvalues, jnp.sum(gradient * unit_v, 0), jnp.sum(gradient, 0))


def contract_rows(left, right):
    return lax.dot_general(left, right, (((0,), (0,)), ((), ())), preferred_element_type=f32)


def contract_cols(left, right):
    return lax.dot_general(left, right, (((1,), (1,)), ((), ())), preferred_element_type=f32)


def join_tp(mine, other, me):
    return jnp.where(me == 0, jnp.concatenate([mine, other], -1), jnp.concatenate([other, mine], -1))


def reach(rows):
    left, out, far = LONGEST, [], 1
    while left > 0:
        out.append((far, min(rows, left)))
        left -= rows
        far += 1
    return out


def body(
    sizes, tokens, segments, cotangent, w_qkv, w_out, w_gate, w_up, w_down, norm_gain, norm_bias, final_gain, final_bias
):
    n_dp, n_ctx, n_tp = sizes
    me_dp, me_ctx, me_tp = lax.axis_index("dp"), lax.axis_index("ctx"), lax.axis_index("tp")
    seqs, rows, width = tokens.shape
    count = seqs * rows
    local = w_qkv.shape[2]
    hidden = w_gate.shape[1]
    own_rows = w_qkv.shape[0]
    window = rows + 2 * LONGEST
    share = width // n_tp
    scalars = jnp.stack([me_dp, me_dp ^ 1, me_dp ^ 2, me_dp ^ 3, me_tp]).astype(jnp.int32)
    direct = n_dp == 4 and own_rows % 32 == 0

    qkv_own = w_qkv.reshape(own_rows, 3 * local)
    steps = reach(rows)
    feature = lambda ref: pl.ds(pl.multiple_of(ref[4] * share, 128), share)
    copies, shapes = [], []
    for far, take in steps:
        for start in (rows - take, 0):
            src = lambda ref, start=start, take=take: (slice(None), pl.ds(start, take), feature(ref))
            copies.append((0, src, len(shapes), lambda ref: (slice(None),) * 3, (seqs, take, share)))
            shapes.append((seqs, take, share))
    gives = move(copies, [tokens], shapes, scalars, "pick_tokens")
    left, right = [], []
    if direct:
        near = sent(qkv_own, "dp", xor_perm(4, 1))
        far_w = sent(qkv_own, "dp", xor_perm(4, 2))
    for n, (far, take) in enumerate(steps):
        left.insert(0, sent(gives[2 * n], "ctx", shift_perm(n_ctx, far)))
        right.append(sent(gives[2 * n + 1], "ctx", shift_perm(n_ctx, -far)))
    docs, bit = segments, 1
    while bit < n_ctx:
        got = sent(docs, "ctx", xor_perm(n_ctx, bit))
        docs = jnp.where((me_ctx & bit) != 0, jnp.concatenate([got, docs], 1), jnp.concatenate([docs, got], 1))
        bit *= 2
    if direct:
        half = own_rows // 2
        top = sent(near[:half], "dp", xor_perm(4, 2))
        low = sent(far_w[half:], "dp", xor_perm(4, 1))
        parts = [qkv_own, near, far_w, top, low]
        plan = [(0, own_rows, 0), (1, own_rows, 0), (2, own_rows, 0), (3, own_rows, 0), (3, own_rows, half)]
    else:
        parts, plan = [gather_rows(qkv_own, me_dp, n_dp)], [(0, 0, 0)]

    lines = jnp.stack([norm_gain, norm_bias, final_gain, final_bias], 1)
    lines = jnp.pad(lines, ((0, 0), (0, 124)))
    cuts = [(0, local), (local, local + 128)]
    for n in range(3):
        cuts.append((cuts[-1][1], cuts[-1][1] + hidden))
    rest_cols = cuts[-1][1]
    owned = [w_out, lines, w_gate, w_up, w_down]
    everything = lambda ref: (slice(None), slice(None))
    if direct:
        (rest,) = move(
            [(n, everything, 0, all_rows(*cut), (own_rows, cut[1] - cut[0])) for n, cut in enumerate(cuts)],
            owned,
            [(own_rows, rest_cols)],
            scalars,
            "pack_weights",
        )
        rest, _ = lax.optimization_barrier((rest, (top, low)))
        got = fetch_rows(rest)
        copies = []
        for n, cut in enumerate(cuts):
            cols = slice(*cut)
            target = lambda k, offset, size: rows_at(k, (own_rows, offset), size)
            copies.append((n, everything, n, target(0, 0, own_rows), (own_rows, cut[1] - cut[0])))
            for g, (k, offset, size) in enumerate(((1, 0, own_rows), (2, 0, own_rows), (3, 0, half), (3, half, half))):
                copies.append(
                    (len(owned) + g, all_rows(*cut), n, target(k, offset, size), (size, cut[1] - cut[0]))
                )
        out_w, lines, gate_w, up_w, down_w = move(
            copies, owned + list(got), [(width, hi - lo) for lo, hi in cuts], scalars, "place_weights"
        )
    else:
        out_w, lines, gate_w, up_w, down_w = [gather_rows(w, me_dp, n_dp) for w in owned]
    params = lines[:, :4].astype(f32).T
    gain_one, bias_one, gain_two, bias_two = params[0], params[1], params[2], params[3]

    quarter = HD // 2
    places = (me_ctx * rows - LONGEST + jnp.arange(window)).astype(f32)
    inverse = rotary_base ** (-(jnp.arange(quarter).astype(f32) * 2.0 / HD))
    angles = places[:, None] * jnp.concatenate([inverse] * 4)[None, :]
    lead = (jnp.arange(128) % HD) < quarter
    cos_t, sine = jnp.cos(angles), jnp.sin(angles)
    sin_a = jnp.where(lead[None, :], -sine, 0.0)
    sin_b = jnp.where(lead[None, :], 0.0, sine)

    offset = LONGEST - me_ctx * rows
    below = jnp.sum(docs[:, None, :] < jnp.arange(9)[None, :, None], -1).astype(jnp.int32)
    is_doc = segments[:, None, :] == jnp.arange(8)[None, :, None]
    begin = jnp.sum(jnp.where(is_doc, below[:, :8, None], 0), 1) + offset
    end = jnp.sum(jnp.where(is_doc, below[:, 1:, None], 0), 1) + offset
    ends = jnp.stack([begin, end], 1)
    spans = []
    for at in range(0, rows, TILE):
        spans += [begin[:, at] // TILE, (end[:, at + TILE - 1] + TILE - 1) // TILE]
    span = jnp.stack(spans, 1)

    shape = Window(seqs, rows, [p.shape[1] for p in left], [p.shape[1] for p in right])
    pieces = []
    for piece in left:
        pieces += [piece, sent(piece, "tp", xor_perm(n_tp, 1))]
    pieces.append(tokens)
    for piece in right:
        pieces += [piece, sent(piece, "tp", xor_perm(n_tp, 1))]
    q, k, v, qkv_w = project(scalars, shape, pieces, parts, plan, cos_t, sin_a, sin_b)
    mixture, logs = attend(span, q, k, v, ends)

    flat = tokens.reshape(count, width)
    mixture_flat = mixture.reshape(count, local)
    attended = add_over_tp(contract_cols(mixture_flat, out_w), n_tp)
    normed, unit_one, inv_one = norm_forward(flat.astype(f32) + attended, gain_one, bias_one)
    normed_low = normed.astype(bf16)
    gate_pre = jnp.dot(normed_low, gate_w, preferred_element_type=f32)
    up_pre = jnp.dot(normed_low, up_w, preferred_element_type=f32)
    sigmoid_g = jax.nn.sigmoid(gate_pre)
    activated = gate_pre * sigmoid_g
    hidden_low = (activated * up_pre).astype(bf16)
    branch = add_over_tp(contract_cols(hidden_low, down_w), n_tp)
    final_out, unit_two, inv_two = norm_forward(normed + branch, gain_two, bias_two)
    output = final_out.astype(bf16).reshape(seqs, rows, width)

    grad_out = cotangent.reshape(count, width).astype(f32)
    dsum, dgain_two, dbias_two = norm_backward(grad_out, unit_two, inv_two, gain_two)
    dbranch = dsum.astype(bf16)
    mine = (me_dp, me_ctx)
    r_down = Reduction(contract_rows(dbranch, hidden_low).astype(bf16), sizes, mine, scalars, "down").first()
    dhidden = jnp.dot(dbranch, down_w, preferred_element_type=f32)
    dgate = (dhidden * up_pre * sigmoid_g * (1.0 + gate_pre * (1.0 - sigmoid_g))).astype(bf16)
    dup = (dhidden * activated).astype(bf16)
    dnormed_part = contract_cols(dgate, gate_w) + contract_cols(dup, up_w)
    dnormed = dsum + add_over_tp(dnormed_part, n_tp)
    r_gate = Reduction(contract_rows(normed_low, dgate).astype(bf16), sizes, mine, scalars, "gate").first()
    r_up = Reduction(contract_rows(normed_low, dup).astype(bf16), sizes, mine, scalars, "up").first()
    dresid, dgain_one, dbias_one = norm_backward(dnormed, unit_one, inv_one, gain_one)
    dattended = dresid.astype(bf16)
    d_out = contract_rows(dattended, mixture_flat).astype(bf16)
    dmixture = jnp.dot(dattended, out_w, preferred_element_type=f32).astype(bf16).reshape(seqs, rows, local)

    token = lambda *steps: [r.token for r in steps if r.direct]
    r_down.second()
    small = total_small(jnp.stack([dgain_one, dbias_one, dgain_two, dbias_two]), me_dp, sizes)
    backs = []
    for seq in range(seqs):
        backs.append(
            attend_back(
                seq, span, q, k, v, ends, mixture, logs, dmixture, cos_t, sin_a, sin_b, token(r_down, r_gate, r_up)
            )
        )
        done = backs[-1][0]
        if seq == 0:
            r_down.inward(done)
            r_gate.second(done)
            r_up.second(done)
    r_down.across(done)
    r_gate.inward(done)
    r_up.inward(done)
    dq, dk, dv = [jnp.concatenate(kind, 0) for kind in zip(*backs)]
    keep, give, d_last = project_back(
        scalars, shape, pieces, dq, dk, dv, qkv_w, d_out, token(r_down, r_gate, r_up)
    )
    r_last = Reduction(d_last, sizes, mine, scalars, "last").first()
    r_down.outward(d_last)
    r_gate.across(d_last)
    r_up.across(d_last)

    dx_half = keep.astype(f32) + sent(give, "tp", xor_perm(n_tp, 1)).astype(f32)
    total = dx_half[:, LONGEST : LONGEST + rows]
    at = LONGEST
    for far, take in steps:
        to_left = dx_half[:, at - take : at].astype(bf16)
        to_right = dx_half[:, window - at : window - at + take].astype(bf16)
        from_right = sent(to_left, "ctx", shift_perm(n_ctx, -far)).astype(f32)
        from_left = sent(to_right, "ctx", shift_perm(n_ctx, far)).astype(f32)
        pad = rows - take
        total = total + jnp.pad(from_right, ((0, 0), (pad, 0), (0, 0))) + jnp.pad(from_left, ((0, 0), (0, pad), (0, 0)))
        at -= take
    r_last.second()
    r_gate.outward()
    r_up.outward()
    r_last.inward().across().outward()
    half_in = total.astype(bf16)
    dinput = join_tp(half_in, sent(half_in, "tp", xor_perm(n_tp, 1)), me_tp).reshape(count, width)
    d_tokens = (dresid + dinput.astype(f32)).astype(bf16).reshape(seqs, rows, width)

    g_last = r_last.result()
    g_qkv = g_last[:, : 3 * local].reshape(own_rows, 3, local)
    g_out = g_last[:, 3 * local :]
    return (
        output,
        d_tokens,
        g_qkv,
        g_out,
        r_gate.result(),
        r_up.result(),
        r_down.result(),
        small[0],
        small[1],
        small[2],
        small[3],
    )


def solution(mesh):
    sizes = (mesh.shape["dp"], mesh.shape["ctx"], mesh.shape["tp"])
    wide, flat, kinds, square, line = (
        P("dp", "ctx", None),
        P("dp", "ctx"),
        P("dp", None, "tp"),
        P("dp", "tp"),
        P("dp"),
    )
    return jax.shard_map(
        functools.partial(body, sizes),
        mesh=mesh,
        in_specs=(wide, flat, wide, kinds) + (square,) * 4 + (line,) * 4,
        out_specs=(wide, wide, kinds) + (square,) * 4 + (line,) * 4,
        check_vma=False,
    )
```

```python
import functools

import jax
import jax.numpy as jnp
from jax import lax
from jax.experimental import pallas as pl
from jax.experimental.pallas import tpu as pltpu
from jax.sharding import PartitionSpec as P

HD = 64
LONGEST = 768
TILE = 256

epsilon = 1e-12
rotary_base = 1000.0
NEG = -1e30
LOG2E = 1.4426950408889634


bf16 = jnp.bfloat16
f32 = jnp.float32


def xor_perm(count, bit):
    return [(i, i ^ bit) for i in range(count)]


def shift_perm(count, by):
    return [(i, i + by) for i in range(count) if 0 <= i + by < count]


def sent(values, axis, perm):
    return lax.ppermute(values, axis, perm)


def move(copies, sources, shapes, scalars, name, after=()):
    count = len(sources)

    def kernel(scalar_ref, *refs):
        given, refs = refs[:count], refs[count + len(after) :]
        made, held, sems_in, sems_out = refs[: len(shapes)], refs[len(shapes) : -2], refs[-2], refs[-1]
        inward = []
        for n, (src, src_at, _, _, _) in enumerate(copies):
            inward.append(pltpu.make_async_copy(given[src].at[src_at(scalar_ref)], held[n], sems_in.at[n]))
            inward[-1].start()
        outward = []
        for n, (_, _, dst, dst_at, _) in enumerate(copies):
            inward[n].wait()
            outward.append(pltpu.make_async_copy(held[n], made[dst].at[dst_at(scalar_ref)], sems_out.at[n]))
            outward[-1].start()
        for copy in outward:
            copy.wait()

    anywhere = pl.BlockSpec(memory_space=pl.ANY)
    return pl.pallas_call(
        kernel,
        grid_spec=pltpu.PrefetchScalarGridSpec(
            num_scalar_prefetch=1,
            grid=(),
            in_specs=[anywhere] * (count + len(after)),
            out_specs=[anywhere] * len(shapes),
            scratch_shapes=[pltpu.VMEM(copy[4], bf16) for copy in copies]
            + [pltpu.SemaphoreType.DMA((len(copies),))] * 2,
        ),
        out_shape=[jax.ShapeDtypeStruct(shape, bf16) for shape in shapes],
        name=name,
    )(scalars, *sources, *after)


def rows_at(index, start, size):
    return lambda ref: (pl.ds(pl.multiple_of(ref[index] * start[0] + start[1], 16), size), slice(None))


def all_rows(*cols):
    cut = slice(*cols) if cols else slice(None)
    return lambda ref: (slice(None), cut)


def gather_rows(own, me, count):
    bit = 1
    while bit < count:
        got = sent(own, "dp", xor_perm(count, bit))
        own = jnp.where((me & bit) != 0, jnp.concatenate([got, own], 0), jnp.concatenate([own, got], 0))
        bit *= 2
    return own


def scatter_rows(grad, me, count):
    bit, grad = count // 2, grad.astype(f32)
    while bit >= 1:
        half = grad.shape[0] // 2
        side = jnp.where((me & bit) != 0, 1, 0)
        give = lax.dynamic_slice_in_dim(grad, (1 - side) * half, half, 0).astype(bf16)
        grad = lax.dynamic_slice_in_dim(grad, side * half, half, 0)
        grad = grad + sent(give, "dp", xor_perm(count, bit)).astype(f32)
        bit //= 2
    return grad.astype(bf16)


def add_kernel(scalar_ref, *refs, rows, terms, stack):
    made = refs[-1:] if stack else refs[-len(terms) :]
    at = 0
    for n, widths in enumerate(terms):
        total = 0.0
        for count in widths:
            parts = [ref[...].astype(f32) for ref in refs[at : at + count]]
            total = total + (parts[0] if count == 1 else jnp.concatenate(parts, 1))
            at += count
        if stack:
            made[0][n * rows : (n + 1) * rows] = total.astype(bf16)
        else:
            made[n][...] = total.astype(bf16)


def add_blocks(scalars, sums, rows, cols, after, name, stack=False):
    outs, height = (1, rows * len(sums)) if stack else (len(sums), rows)
    specs, values, terms = [], [], []
    for parts in sums:
        terms.append([len(arrays) for arrays, _ in parts])
        for arrays, index in parts:
            at = (lambda c, ref, index=index: (index(ref), 0)) if callable(index) else (lambda c, ref, index=index: (index, 0))
            for array in arrays:
                specs.append(pl.BlockSpec((rows, array.shape[1]), at))
                values.append(array)
    anywhere = pl.BlockSpec(memory_space=pl.ANY)
    return pl.pallas_call(
        functools.partial(add_kernel, rows=rows, terms=terms, stack=stack),
        grid_spec=pltpu.PrefetchScalarGridSpec(
            num_scalar_prefetch=1,
            grid=(1,),
            in_specs=specs + [anywhere] * len(after),
            out_specs=[pl.BlockSpec((height, cols), lambda c, ref: (0, 0))] * outs,
        ),
        out_shape=[jax.ShapeDtypeStruct((height, cols), bf16)] * outs,
        name=name,
    )(scalars, *values, *after)


class Reduction:
    def __init__(self, grads, sizes, mine, scalars, name):
        self.grads, self.name, self.scalars = grads, name, scalars
        self.n_dp, self.n_ctx, _ = sizes
        self.me_dp, self.me_ctx = mine
        self.rows, self.cols = grads[0].shape[0] // self.n_dp, sum(g.shape[1] for g in grads)
        self.half = self.rows // 2
        self.direct = self.n_dp == 4 and self.half % 16 == 0

    def first(self):
        if not self.direct:
            self.part = scatter_rows(jnp.concatenate(self.grads, 1), self.me_dp, self.n_dp)
            return self
        rows, half = self.rows, self.half
        copies, col = [], 0
        for n, grad in enumerate(self.grads):
            for k, offset, which, start in ((3, 0, 0, 0), (3, half, 1, 0), (1, 0, 0, half), (2, half, 1, half)):
                target = lambda ref, start=start, col=col, wide=grad.shape[1]: (pl.ds(start, half), pl.ds(col, wide))
                copies.append((n, rows_at(k, (rows, offset), half), which, target, (half, grad.shape[1])))
            col += grad.shape[1]
        x_give, y_give = move(copies, self.grads, [(rows, self.cols)] * 2, self.scalars, "pick_" + self.name)
        self.token = x_give
        self.x_got = sent(x_give, "dp", xor_perm(4, 1))
        self.y_got = sent(y_give, "dp", xor_perm(4, 2))
        return self

    def second(self, *after):
        if not self.direct:
            return self
        x_next, y_next = add_blocks(
            self.scalars,
            [
                [(self.grads, lambda ref: ref[1] * 2 + 1), ([self.y_got], 0)],
                [(self.grads, lambda ref: ref[2] * 2), ([self.x_got], 0)],
            ],
            self.half,
            self.cols,
            after,
            "add_second_" + self.name,
        )
        self.token = x_next
        self.x_last = sent(x_next, "dp", xor_perm(4, 1))
        self.y_last = sent(y_next, "dp", xor_perm(4, 2))
        return self

    def inward(self, *after):
        if self.direct:
            (self.part,) = add_blocks(
                self.scalars,
                [
                    [(self.grads, lambda ref: ref[0] * 2), ([self.x_got], 1), ([self.y_last], 0)],
                    [(self.grads, lambda ref: ref[0] * 2 + 1), ([self.y_got], 1), ([self.x_last], 0)],
                ],
                self.half,
                self.cols,
                after,
                "add_inward_" + self.name,
                stack=True,
            )
        if self.n_ctx == 4:
            self.got = sent(self.part, "ctx", [(0, 1), (3, 2)])
        self.token = self.part
        return self

    def plus(self, name, after):
        if self.rows % 16 == 0 and after:
            (self.part,) = add_blocks(
                self.scalars, [[([self.part], 0), ([self.got], 0)]], self.rows, self.cols, after, name + self.name
            )
        else:
            self.part = (self.part.astype(f32) + self.got.astype(f32)).astype(bf16)
        self.token = self.part

    def across(self, *after):
        if self.n_ctx == 4:
            self.plus("add_across_", after)
            self.got = sent(self.part, "ctx", [(1, 2), (2, 1)])
        return self

    def outward(self, *after):
        if self.n_ctx == 4:
            self.plus("add_outward_", after)
            self.got = sent(self.part, "ctx", [(1, 0), (2, 3)])
        return self

    def result(self):
        if self.n_ctx == 4:
            edge = (self.me_ctx == 0) | (self.me_ctx == 3)
            return jnp.where(edge, self.got, self.part).astype(f32)
        part, bit = self.part, 1
        while bit < self.n_ctx:
            got = sent(part, "ctx", xor_perm(self.n_ctx, bit))
            part = (part.astype(f32) + got.astype(f32)).astype(bf16)
            bit *= 2
        return part.astype(f32)


def place_kernel(scalar_ref, *refs):
    rows = refs[0].shape[0]
    for k in range(4):
        refs[4][pl.ds(pl.multiple_of((scalar_ref[5] ^ k) * rows, 16), rows), :] = refs[k][...].astype(f32)


def reduce_last(blocks, sizes, mine, scalars):
    me_ctx = mine[1]
    total = blocks[0].astype(f32)
    for k in range(1, 4):
        total = total + sent(blocks[k], "dp", xor_perm(4, k)).astype(f32)
    low = total.astype(bf16)
    rows = low.shape[0] // 4
    piece = lambda k: lax.dynamic_slice_in_dim(low, (me_ctx ^ k) * rows, rows, 0)
    summed = piece(0).astype(f32)
    for k in range(1, 4):
        summed = summed + sent(piece(k), "ctx", xor_perm(4, k)).astype(f32)
    own = summed.astype(bf16)
    parts = [own] + [sent(own, "ctx", xor_perm(4, k)) for k in range(1, 4)]
    return pl.pallas_call(
        place_kernel,
        grid_spec=pltpu.PrefetchScalarGridSpec(
            num_scalar_prefetch=1,
            grid=(1,),
            in_specs=[pl.BlockSpec(own.shape, lambda c, ref: (0, 0))] * 4,
            out_specs=pl.BlockSpec(low.shape, lambda c, ref: (0, 0)),
        ),
        out_shape=jax.ShapeDtypeStruct(low.shape, f32),
        name="place_last",
    )(scalars, *parts)


def add_over_tp(part, count):
    low = part.astype(bf16)
    bit = 1
    total = low
    while bit < count:
        got = lax.ppermute(total, "tp", xor_perm(count, bit))
        total = total.astype(f32) + got.astype(f32)
        bit *= 2
    return total.astype(f32)


def turn(values, cosine, sine_a, sine_b):
    width = values.shape[-1]
    ahead = pltpu.roll(values, width - HD // 2, 1)
    behind = pltpu.roll(values, HD // 2, 1)
    return values * cosine + ahead * sine_a + behind * sine_b


class Window:
    def __init__(self, seqs, rows, pieces_left, pieces_right):
        self.parts = []
        at = 0
        for kind, sizes in (("left", pieces_left), ("own", [rows]), ("right", pieces_right)):
            for n, size in enumerate(sizes):
                self.parts.append((kind, at, at + size // TILE))
                at += size // TILE
        self.blocks = at
        self.first, self.last = next((lo, hi) for kind, lo, hi in self.parts if kind == "own")

    def own_block(self, b):
        return jnp.clip(b - self.first, 0, self.last - self.first - 1)

    def specs(self, width):
        out = []
        for kind, lo, hi in self.parts:
            at = lambda s, b, *ref, lo=lo, hi=hi: (s, jnp.clip(b - lo, 0, hi - lo - 1), 0)
            if kind == "own":
                out.append(pl.BlockSpec((1, TILE, width), at))
            else:
                out += [pl.BlockSpec((1, TILE, width // 2), at)] * 2
        return out

    def visit(self, refs, block, emit):
        at = 0
        for kind, lo, hi in self.parts:
            mine = refs[at : at + (1 if kind == "own" else 2)]
            at += len(mine)

            @pl.when((block >= lo) & (block < hi))
            def _():
                emit([ref[0] for ref in mine])


def project_kernel(scalar_ref, *refs, shape, pieces, plan):
    rows_in = refs[:pieces]
    weights = refs[pieces : pieces + len(plan)]
    cos_ref, sa_ref, sb_ref, q_ref, k_ref, v_ref, w_ref, x_ref = refs[pieces + len(plan) :]
    width = k_ref.shape[2]
    core = scalar_ref[4]

    @pl.when((pl.program_id(0) == 0) & (pl.program_id(1) == 0))
    def _():
        for ref, (index, size, offset) in zip(weights, plan):
            rows = ref.shape[0]
            w_ref[pl.ds(pl.multiple_of(scalar_ref[index] * size + offset, 16), rows), :] = ref[...]

    cosine, sine_a, sine_b = cos_ref[...], sa_ref[...], sb_ref[...]

    def emit(parts):
        full = len(parts) == 1
        half = w_ref.shape[0] // 2
        if full:
            rows = parts[0]
            x_ref[0] = rows
        else:
            x_ref[0, :, pl.ds(pl.multiple_of(core * half, 128), half)] = parts[0]
            x_ref[0, :, pl.ds(pl.multiple_of((1 - core) * half, 128), half)] = parts[1]
            rows = x_ref[0]
        for kind, ref in ((0, q_ref), (1, k_ref), (2, v_ref)):
            if kind == 0 and not full:
                continue
            out = jnp.dot(rows, w_ref[:, kind * width : (kind + 1) * width], preferred_element_type=f32)
            if kind == 2:
                ref[0] = out.astype(bf16)
            else:
                for at in range(0, width, 128):
                    ref[0, :, at : at + 128] = turn(out[:, at : at + 128], cosine, sine_a, sine_b).astype(bf16)

    shape.visit(rows_in, pl.program_id(1), emit)


def project(scalars, shape, pieces, parts, plan, cosine, sine_a, sine_b):
    own = next(p for p, (kind, _, _) in zip(group(shape, pieces), shape.parts) if kind == "own")[0]
    seqs, rows, width = own.shape
    local = parts[0].shape[1] // 3
    window = shape.blocks * TILE
    table = pl.BlockSpec((TILE, 128), lambda s, b, ref: (b, 0))
    whole = lambda array: pl.BlockSpec(array.shape, lambda s, b, ref: (0, 0))
    return pl.pallas_call(
        functools.partial(project_kernel, shape=shape, pieces=len(pieces), plan=plan),
        grid_spec=pltpu.PrefetchScalarGridSpec(
            num_scalar_prefetch=1,
            grid=(seqs, shape.blocks),
            in_specs=shape.specs(width) + [whole(p) for p in parts] + [table] * 3,
            out_specs=[
                pl.BlockSpec((1, TILE, local), lambda s, b, ref: (s, shape.own_block(b), 0)),
                pl.BlockSpec((1, TILE, local), lambda s, b, ref: (s, b, 0)),
                pl.BlockSpec((1, TILE, local), lambda s, b, ref: (s, b, 0)),
                pl.BlockSpec((width, 3 * local), lambda s, b, ref: (0, 0)),
                pl.BlockSpec((1, TILE, width), lambda s, b, ref: (s, b, 0)),
            ],
        ),
        out_shape=[
            jax.ShapeDtypeStruct((seqs, rows, local), bf16),
            jax.ShapeDtypeStruct((seqs, window, local), bf16),
            jax.ShapeDtypeStruct((seqs, window, local), bf16),
            jax.ShapeDtypeStruct((width, 3 * local), bf16),
            jax.ShapeDtypeStruct((seqs, window, width), bf16),
        ],
        cost_estimate=pl.CostEstimate(flops=6 << 30, transcendentals=0, bytes_accessed=16 << 20),
        name="project",
    )(scalars, *pieces, *parts, cosine, sine_a, sine_b)


def group(shape, pieces):
    out, at = [], 0
    for kind, _, _ in shape.parts:
        size = 1 if kind == "own" else 2
        out.append(pieces[at : at + size])
        at += size
    return out


BACK = 512


def project_back_kernel(scalar_ref, *refs, first, blocks, carried, given):
    x_ref, dq_ref, dk_ref, dv_ref, w_ref = refs[:5]
    outs = refs[given:]
    keep_ref, give_ref, made, acc_ref = outs[0], outs[1], outs[2:-1], outs[-1]
    width = dk_ref.shape[2]
    core = scalar_ref[4]
    half = w_ref.shape[0] // 2
    block = pl.program_id(0)
    rows = dq_ref.shape[1]

    @pl.when(block == 0)
    def _():
        acc_ref[...] = refs[5][...] if carried else jnp.zeros_like(acc_ref)

    grads = [(1, dk_ref[0]), (2, dv_ref[0])]
    cols = lambda kind: slice(kind * width, (kind + 1) * width)
    places = ((keep_ref, pl.multiple_of(core * half, 16)), (give_ref, pl.multiple_of((1 - core) * half, 16)))
    totals = []
    for _, at in places:
        total = across(grads[0][1], w_ref[pl.ds(at, half), cols(1)])
        totals.append(total + across(grads[1][1], w_ref[pl.ds(at, half), cols(2)]))
    for kind, grad in grads:
        acc_ref[:, cols(kind)] += contract_rows(x_ref[0], grad)
    for (out_ref, _), total in zip(places, totals):
        out_ref[0] = total.astype(bf16)
    for n in range(blocks):
        low, high = max(first, n * BACK), min(first + rows, (n + 1) * BACK)
        if low >= high:
            continue

        @pl.when(block == n)
        def _():
            here = slice(low - n * BACK, high - n * BACK)
            grad = dq_ref[0, low - first : high - first, :]
            acc_ref[:, cols(0)] += contract_rows(x_ref[0, here, :], grad)
            for (out_ref, at), total in zip(places, totals):
                more = across(grad, w_ref[pl.ds(at, half), cols(0)])
                out_ref[0, here, :] = (total[here] + more).astype(bf16)

    @pl.when(block == blocks - 1)
    def _():
        if len(made) == 1:
            made[0][...] = acc_ref[...].astype(made[0].dtype)
        else:
            size = made[0].shape[0]
            for k, ref in enumerate(made):
                ref[...] = acc_ref[pl.ds(pl.multiple_of(scalar_ref[k] * size, 16), size), :].astype(bf16)


def project_back(seq, scalars, x, dq, dk, dv, weight, carry, parts, after):
    _, window, local = dk.shape
    rows, width = dq.shape[1], weight.shape[0]
    blocks = window // BACK
    row = lambda size: pl.BlockSpec((1, BACK, size), lambda b, ref: (0, b, 0))
    whole = lambda shape: pl.BlockSpec(shape, lambda b, ref: (0, 0))
    extra = [] if carry is None else [carry]
    if parts is None:
        made = [jax.ShapeDtypeStruct((width, 3 * local), f32)]
    elif parts == 1:
        made = [jax.ShapeDtypeStruct((width, 3 * local), bf16)]
    else:
        made = [jax.ShapeDtypeStruct((width // parts, 3 * local), bf16)] * parts
    return pl.pallas_call(
        functools.partial(
            project_back_kernel,
            first=(window - rows) // 2,
            blocks=blocks,
            carried=carry is not None,
            given=5 + len(extra) + len(after),
        ),
        grid_spec=pltpu.PrefetchScalarGridSpec(
            num_scalar_prefetch=1,
            grid=(blocks,),
            in_specs=[
                pl.BlockSpec((1, BACK, width), lambda b, ref: (seq, b, 0)),
                pl.BlockSpec((1, rows, local), lambda b, ref: (0, 0, 0)),
                row(local),
                row(local),
                whole(weight.shape),
            ]
            + [whole(c.shape) for c in extra]
            + [pl.BlockSpec(memory_space=pl.ANY)] * len(after),
            out_specs=[row(width // 2), row(width // 2)] + [whole(m.shape) for m in made],
            scratch_shapes=[pltpu.VMEM((width, 3 * local), f32)],
        ),
        out_shape=[jax.ShapeDtypeStruct((1, window, width // 2), bf16)] * 2 + made,
        cost_estimate=pl.CostEstimate(flops=6 << 30, transcendentals=0, bytes_accessed=16 << 20),
        name="project_back",
    )(scalars, x, dq, dk, dv, weight, *extra, *after)


def head_lanes(values, head):
    lane = lax.broadcasted_iota(jnp.int32, values.shape, 1)
    inside = (lane < HD) if head == 0 else (lane >= HD)
    return jnp.where(inside, values, jnp.zeros_like(values))


def across(left, right):
    return lax.dot_general(left, right, (((1,), (1,)), ((), ())), preferred_element_type=f32)


def pair_of(head):
    return slice(head // 2 * 128, head // 2 * 128 + 128)


def attend_kernel(span_ref, q_ref, k_ref, v_ref, ends_ref, o_ref, l_ref, acc_ref):
    seq, blk = pl.program_id(0), pl.program_id(1)
    heads = q_ref.shape[2] // HD
    scale = HD**-0.5 * LOG2E
    query = q_ref[0]
    queries = [head_lanes(query[:, pair_of(h)], h % 2) for h in range(heads)]
    begin, end = ends_ref[0, 0:1, :], ends_ref[0, 1:2, :]
    acc_ref[...] = jnp.zeros_like(acc_ref)

    def step(j, carry):
        start = pl.multiple_of(j * TILE, TILE)
        place = lax.broadcasted_iota(jnp.int32, (TILE, TILE), 0) + start
        same = (place >= begin) & (place < end)
        out = []
        for h in range(heads):
            largest, total = carry[h]
            if h % 2 == 0:
                keys = k_ref[0, pl.ds(start, TILE), pair_of(h)]
                turned = v_ref[0, pl.ds(start, TILE), pair_of(h)].T
            scores = jnp.where(same, across(keys, queries[h]) * scale, NEG)
            bigger = jnp.maximum(largest, jnp.max(scores, 0, keepdims=True))
            probs = jnp.exp2(scores - bigger)
            shrink = jnp.exp2(largest - bigger)
            total = total * shrink + jnp.sum(probs, 0, keepdims=True)
            rows = slice(h * HD, (h + 1) * HD)
            more = jnp.dot(turned[h % 2 * HD : (h % 2 + 1) * HD], probs.astype(bf16), preferred_element_type=f32)
            acc_ref[rows, :] = acc_ref[rows, :] * shrink + more
            out.append((bigger, total))
        return tuple(out)

    fresh = (jnp.full((1, TILE), NEG, f32), jnp.zeros((1, TILE), f32))
    done = lax.fori_loop(span_ref[seq, 2 * blk], span_ref[seq, 2 * blk + 1], step, (fresh,) * heads)
    for h in range(heads):
        largest, total = done[h]
        rows = slice(h * HD, (h + 1) * HD)
        acc_ref[rows, :] = acc_ref[rows, :] / total
        l_ref[0, h : h + 1, :] = largest + jnp.log2(total)
    for h in range(0, heads, 2):
        o_ref[0, :, pair_of(h)] = acc_ref[h * HD : (h + 2) * HD, :].T.astype(bf16)


def attend(span, q, k, v, ends):
    seqs, rows, local = q.shape
    window = k.shape[1]
    mine = pl.BlockSpec((1, TILE, local), lambda s, b, span: (s, b, 0))
    whole = pl.BlockSpec((1, window, local), lambda s, b, span: (s, 0, 0))
    line = lambda size: pl.BlockSpec((1, size, TILE), lambda s, b, span: (s, 0, b))
    return pl.pallas_call(
        attend_kernel,
        grid_spec=pltpu.PrefetchScalarGridSpec(
            num_scalar_prefetch=1,
            grid=(seqs, rows // TILE),
            in_specs=[mine, whole, whole, line(2)],
            out_specs=[mine, line(local // HD)],
            scratch_shapes=[pltpu.VMEM((local, TILE), f32)],
        ),
        out_shape=[
            jax.ShapeDtypeStruct((seqs, rows, local), bf16),
            jax.ShapeDtypeStruct((seqs, local // HD, rows), f32),
        ],
        cost_estimate=pl.CostEstimate(flops=8 << 30, transcendentals=8 << 20, bytes_accessed=8 << 20),
        name="attend",
    )(span, q, k, v, ends)


def attend_back_kernel(
    span_ref, q_ref, k_ref, v_ref, ends_ref, o_ref, l_ref, g_ref, cos_ref, sa_ref, sb_ref, *rest, first, seq, blocks
):
    dq_ref, dk_ref, dv_ref, dq_acc, dk_acc, dv_acc = rest[-6:]
    blk = pl.program_id(0)
    heads = q_ref.shape[2] // HD
    window = k_ref.shape[1]
    factor = HD**-0.5
    scale = factor * LOG2E

    @pl.when(blk == 0)
    def _():
        dk_acc[...] = jnp.zeros_like(dk_acc)
        dv_acc[...] = jnp.zeros_like(dv_acc)

    dq_acc[...] = jnp.zeros_like(dq_acc)
    query, grad = q_ref[0], g_ref[0]
    queries = [head_lanes(query[:, pair_of(h)], h % 2) for h in range(heads)]
    grads = [head_lanes(grad[:, pair_of(h)], h % 2) for h in range(heads)]
    product = (grad.astype(f32) * o_ref[0].astype(f32)).T
    deltas = [jnp.sum(product[h * HD : (h + 1) * HD], 0, keepdims=True) for h in range(heads)]
    logs = [l_ref[0, h : h + 1, :] for h in range(heads)]
    begin, end = ends_ref[0, 0:1, :], ends_ref[0, 1:2, :]

    def step(j, carry):
        start = pl.multiple_of(j * TILE, TILE)
        place = lax.broadcasted_iota(jnp.int32, (TILE, TILE), 0) + start
        same = (place >= begin) & (place < end)
        for h in range(0, heads, 2):
            lanes = pair_of(h)
            keys = k_ref[0, pl.ds(start, TILE), lanes]
            vals = v_ref[0, pl.ds(start, TILE), lanes]
            turned = keys.T
            dv, dk = [], []
            for n in (h, h + 1):
                scores = jnp.where(same, across(keys, queries[n]) * scale, NEG)
                probs = jnp.exp2(scores - logs[n])
                dprobs = across(vals, grads[n])
                dscores = (probs * (dprobs - deltas[n])).astype(bf16)
                dv.append(jnp.dot(probs.astype(bf16), grads[n], preferred_element_type=f32))
                dk.append(jnp.dot(dscores, queries[n], preferred_element_type=f32))
                rows = slice(n * HD, (n + 1) * HD)
                dq_acc[rows, :] += jnp.dot(
                    turned[n % 2 * HD : (n % 2 + 1) * HD], dscores, preferred_element_type=f32
                )
            dv_acc[pl.ds(start, TILE), lanes] += dv[0] + dv[1]
            dk_acc[pl.ds(start, TILE), lanes] += dk[0] + dk[1]
        return carry

    lax.fori_loop(span_ref[seq, 2 * blk], span_ref[seq, 2 * blk + 1], step, 0)
    row = pl.multiple_of(first + blk * TILE, TILE)
    cosine, sine_a, sine_b = [ref[pl.ds(row, TILE), :] for ref in (cos_ref, sa_ref, sb_ref)]
    for h in range(0, heads, 2):
        dq = dq_acc[h * HD : (h + 2) * HD, :].T * factor
        dq_ref[0, :, pair_of(h)] = turn(dq, cosine, -sine_a, -sine_b).astype(bf16)

    @pl.when(blk == blocks - 1)
    def _():
        def finish(n, carry):
            at = pl.ds(pl.multiple_of(n * TILE, TILE), TILE)
            cosine, sine_a, sine_b = [ref[at, :] for ref in (cos_ref, sa_ref, sb_ref)]
            for h in range(0, heads, 2):
                lanes = pair_of(h)
                dk_ref[0, at, lanes] = turn(dk_acc[at, lanes] * factor, cosine, -sine_a, -sine_b).astype(bf16)
                dv_ref[0, at, lanes] = dv_acc[at, lanes].astype(bf16)
            return carry

        lax.fori_loop(0, window // TILE, finish, 0)


def attend_back(seq, span, q, k, v, ends, out, logs, grad, cosine, sine_a, sine_b, after):
    _, rows, local = q.shape
    window = k.shape[1]
    mine = pl.BlockSpec((1, TILE, local), lambda b, span: (seq, b, 0))
    whole = pl.BlockSpec((1, window, local), lambda b, span: (seq, 0, 0))
    line = lambda size: pl.BlockSpec((1, size, TILE), lambda b, span: (seq, 0, b))
    made = pl.BlockSpec((1, window, local), lambda b, span: (0, 0, 0))
    table = pl.BlockSpec((window, 128), lambda b, span: (0, 0))
    return pl.pallas_call(
        functools.partial(attend_back_kernel, first=(window - rows) // 2, seq=seq, blocks=rows // TILE),
        grid_spec=pltpu.PrefetchScalarGridSpec(
            num_scalar_prefetch=1,
            grid=(rows // TILE,),
            in_specs=[mine, whole, whole, line(2), mine, line(local // HD), mine, table, table, table]
            + [pl.BlockSpec(memory_space=pl.ANY)] * len(after),
            out_specs=[pl.BlockSpec((1, TILE, local), lambda b, span: (0, b, 0)), made, made],
            scratch_shapes=[
                pltpu.VMEM((local, TILE), f32),
                pltpu.VMEM((window, local), f32),
                pltpu.VMEM((window, local), f32),
            ],
        ),
        out_shape=[
            jax.ShapeDtypeStruct((1, rows, local), bf16),
            jax.ShapeDtypeStruct((1, window, local), bf16),
            jax.ShapeDtypeStruct((1, window, local), bf16),
        ],
        cost_estimate=pl.CostEstimate(flops=12 << 30, transcendentals=4 << 20, bytes_accessed=8 << 20),
        name="attend_back",
    )(span, q, k, v, ends, out, logs, grad, cosine, sine_a, sine_b, *after)


def norm_forward(values, gain_v, bias_v):
    average = jnp.mean(values, -1, keepdims=True)
    centred = values - average
    inv_std = lax.rsqrt(jnp.mean(centred * centred, -1, keepdims=True) + epsilon)
    unit_v = centred * inv_std
    return (unit_v * gain_v + bias_v, unit_v, inv_std)


def norm_backward(gradient, unit_v, inv_std, gain_v):
    scaled = gradient * gain_v
    dvalues = (
        scaled
        - jnp.mean(scaled, -1, keepdims=True)
        - unit_v * jnp.mean(scaled * unit_v, -1, keepdims=True)
    ) * inv_std
    return (dvalues, jnp.sum(gradient * unit_v, 0), jnp.sum(gradient, 0))


def contract_rows(left, right):
    return lax.dot_general(left, right, (((0,), (0,)), ((), ())), preferred_element_type=f32)


def contract_cols(left, right):
    return lax.dot_general(left, right, (((1,), (1,)), ((), ())), preferred_element_type=f32)


def join_tp(mine, other, me):
    return jnp.where(me == 0, jnp.concatenate([mine, other], -1), jnp.concatenate([other, mine], -1))


def reach(rows):
    left, out, far = LONGEST, [], 1
    while left > 0:
        out.append((far, min(rows, left)))
        left -= rows
        far += 1
    return out


def body(
    sizes, tokens, segments, cotangent, w_qkv, w_out, w_gate, w_up, w_down, norm_gain, norm_bias, final_gain, final_bias
):
    n_dp, n_ctx, n_tp = sizes
    me_dp, me_ctx, me_tp = lax.axis_index("dp"), lax.axis_index("ctx"), lax.axis_index("tp")
    seqs, rows, width = tokens.shape
    count = seqs * rows
    local = w_qkv.shape[2]
    hidden = w_gate.shape[1]
    own_rows = w_qkv.shape[0]
    window = rows + 2 * LONGEST
    share = width // n_tp
    scalars = jnp.stack([me_dp, me_dp ^ 1, me_dp ^ 2, me_dp ^ 3, me_tp, me_ctx]).astype(jnp.int32)
    direct = n_dp == 4 and own_rows % 32 == 0

    qkv_own = w_qkv.reshape(own_rows, 3 * local)
    steps = reach(rows)
    feature = lambda ref: pl.ds(pl.multiple_of(ref[4] * share, 128), share)
    copies, shapes = [], []
    for far, take in steps:
        for start in (rows - take, 0):
            src = lambda ref, start=start, take=take: (slice(None), pl.ds(start, take), feature(ref))
            copies.append((0, src, len(shapes), lambda ref: (slice(None),) * 3, (seqs, take, share)))
            shapes.append((seqs, take, share))
    gives = move(copies, [tokens], shapes, scalars, "pick_tokens")
    left, right = [], []
    docs = jnp.zeros((seqs, n_ctx * rows), jnp.int32)
    for k in range(n_ctx):
        got = segments if k == 0 else sent(segments, "ctx", xor_perm(n_ctx, k))
        docs = lax.dynamic_update_slice_in_dim(docs, got, (me_ctx ^ k) * rows, 1)
    if direct:
        near = sent(qkv_own, "dp", xor_perm(4, 1))
        far_w = sent(qkv_own, "dp", xor_perm(4, 2))
    for n, (far, take) in enumerate(steps):
        left.insert(0, sent(gives[2 * n], "ctx", shift_perm(n_ctx, far)))
        right.append(sent(gives[2 * n + 1], "ctx", shift_perm(n_ctx, -far)))
    if direct:
        half = own_rows // 2
        top = sent(near[:half], "dp", xor_perm(4, 2))
        low = sent(far_w[half:], "dp", xor_perm(4, 1))
        parts = [qkv_own, near, far_w, top, low]
        plan = [(0, own_rows, 0), (1, own_rows, 0), (2, own_rows, 0), (3, own_rows, 0), (3, own_rows, half)]
    else:
        parts, plan = [gather_rows(qkv_own, me_dp, n_dp)], [(0, 0, 0)]

    lines = jnp.stack([norm_gain, norm_bias, final_gain, final_bias], 1)
    lines = jnp.pad(lines, ((0, 0), (0, 124)))
    cuts = [(0, local), (local, local + 128)]
    for n in range(3):
        cuts.append((cuts[-1][1], cuts[-1][1] + hidden))
    rest_cols = cuts[-1][1]
    owned = [w_out, lines, w_gate, w_up, w_down]
    everything = lambda ref: (slice(None), slice(None))
    if direct:
        (rest,) = move(
            [(n, everything, 0, all_rows(*cut), (own_rows, cut[1] - cut[0])) for n, cut in enumerate(cuts)],
            owned,
            [(own_rows, rest_cols)],
            scalars,
            "pack_weights",
        )
        rest, _ = lax.optimization_barrier((rest, (top, low)))
        rest_near = sent(rest, "dp", xor_perm(4, 1))
        rest_far = sent(rest, "dp", xor_perm(4, 2))

    quarter = HD // 2
    places = (me_ctx * rows - LONGEST + jnp.arange(window)).astype(f32)
    inverse = rotary_base ** (-(jnp.arange(quarter).astype(f32) * 2.0 / HD))
    angles = places[:, None] * jnp.concatenate([inverse] * 4)[None, :]
    lead = (jnp.arange(128) % HD) < quarter
    cos_t, sine = jnp.cos(angles), jnp.sin(angles)
    sin_a = jnp.where(lead[None, :], -sine, 0.0)
    sin_b = jnp.where(lead[None, :], 0.0, sine)

    offset = LONGEST - me_ctx * rows
    below = jnp.sum(docs[:, None, :] < jnp.arange(9)[None, :, None], -1).astype(jnp.int32)
    is_doc = segments[:, None, :] == jnp.arange(8)[None, :, None]
    begin = jnp.sum(jnp.where(is_doc, below[:, :8, None], 0), 1) + offset
    end = jnp.sum(jnp.where(is_doc, below[:, 1:, None], 0), 1) + offset
    ends = jnp.stack([begin, end], 1)
    spans = []
    for at in range(0, rows, TILE):
        spans += [begin[:, at] // TILE, (end[:, at + TILE - 1] + TILE - 1) // TILE]
    span = jnp.stack(spans, 1)

    shape = Window(seqs, rows, [p.shape[1] for p in left], [p.shape[1] for p in right])
    pieces = []
    for piece in left:
        pieces += [piece, sent(piece, "tp", xor_perm(n_tp, 1))]
    pieces.append(tokens)
    for piece in right:
        pieces += [piece, sent(piece, "tp", xor_perm(n_tp, 1))]
    q, k, v, qkv_w, x_window = project(scalars, shape, pieces, parts, plan, cos_t, sin_a, sin_b)
    if direct:
        part = lambda start: lambda ref: (pl.ds(start, half), slice(None))
        give_top, give_low = move(
            [(0, part(0), 0, everything, (half, rest_cols)), (1, part(half), 1, everything, (half, rest_cols))],
            [rest_near, rest_far],
            [(half, rest_cols)] * 2,
            scalars,
            "pick_weights",
            after=(q,),
        )
        rest_top = sent(give_top, "dp", xor_perm(4, 2))
        rest_low = sent(give_low, "dp", xor_perm(4, 1))
    mixture, logs = attend(span, q, k, v, ends)

    if direct:
        copies = []
        for n, cut in enumerate(cuts):
            cols = slice(*cut)
            target = lambda k, offset, size: rows_at(k, (own_rows, offset), size)
            copies.append((n, everything, n, target(0, 0, own_rows), (own_rows, cut[1] - cut[0])))
            for g, (who, offset, size) in enumerate(((1, 0, own_rows), (2, 0, own_rows), (3, 0, half), (3, half, half))):
                copies.append(
                    (len(owned) + g, all_rows(*cut), n, target(who, offset, size), (size, cut[1] - cut[0]))
                )
        out_w, lines, gate_w, up_w, down_w = move(
            copies, owned + [rest_near, rest_far, rest_top, rest_low], [(width, hi - lo) for lo, hi in cuts], scalars, "place_weights"
        )
    else:
        out_w, lines, gate_w, up_w, down_w = [gather_rows(w, me_dp, n_dp) for w in owned]
    params = lines[:, :4].astype(f32).T
    gain_one, bias_one, gain_two, bias_two = params[0], params[1], params[2], params[3]
    flat = tokens.reshape(count, width)
    mixture_flat = mixture.reshape(count, local)
    attended = add_over_tp(contract_cols(mixture_flat, out_w), n_tp)
    normed, unit_one, inv_one = norm_forward(flat.astype(f32) + attended, gain_one, bias_one)
    normed_low = normed.astype(bf16)
    gate_pre = jnp.dot(normed_low, gate_w, preferred_element_type=f32)
    up_pre = jnp.dot(normed_low, up_w, preferred_element_type=f32)
    sigmoid_g = jax.nn.sigmoid(gate_pre)
    activated = gate_pre * sigmoid_g
    hidden_low = (activated * up_pre).astype(bf16)
    branch = add_over_tp(contract_cols(hidden_low, down_w), n_tp)
    final_out, unit_two, inv_two = norm_forward(normed + branch, gain_two, bias_two)
    output = final_out.astype(bf16).reshape(seqs, rows, width)

    grad_out = cotangent.reshape(count, width).astype(f32)
    dsum, dgain_two, dbias_two = norm_backward(grad_out, unit_two, inv_two, gain_two)
    dbranch = dsum.astype(bf16)
    mine = (me_dp, me_ctx)
    reduction = lambda grads, name: Reduction(grads, sizes, mine, scalars, name).first()
    r_down = reduction([contract_rows(dbranch, hidden_low).astype(bf16)], "down")
    dhidden = jnp.dot(dbranch, down_w, preferred_element_type=f32)
    dgate = (dhidden * up_pre * sigmoid_g * (1.0 + gate_pre * (1.0 - sigmoid_g))).astype(bf16)
    dup = (dhidden * activated).astype(bf16)
    dnormed_part = contract_cols(dgate, gate_w) + contract_cols(dup, up_w)
    dnormed = dsum + add_over_tp(dnormed_part, n_tp)
    r_gate = reduction([contract_rows(normed_low, dgate).astype(bf16)], "gate")
    d_up = contract_rows(normed_low, dup).astype(bf16)
    dresid, dgain_one, dbias_one = norm_backward(dnormed, unit_one, inv_one, gain_one)
    dattended = dresid.astype(bf16)
    d_out = contract_rows(dattended, mixture_flat).astype(bf16)
    dmixture = jnp.dot(dattended, out_w, preferred_element_type=f32).astype(bf16).reshape(seqs, rows, local)
    lines = jnp.stack([dgain_one, dbias_one, dgain_two, dbias_two], 1)
    lines = jnp.pad(lines, ((0, 0), (0, 124))).astype(bf16)
    r_up = reduction([d_up, d_out, lines], "up")

    tokens_of = lambda *steps: [r.token for r in steps if r.direct]
    half_sums, carry = [], None
    for seq in range(seqs):
        final = seq == seqs - 1
        if seq == 0:
            r_down.second()
        dq, dk, dv = attend_back(
            seq, span, q, k, v, ends, mixture, logs, dmixture, cos_t, sin_a, sin_b, tokens_of(r_down, r_gate, r_up)
        )
        if seq == 0:
            r_down.inward(dq)
            r_gate.second(dq)
            r_up.second(dq)
        elif seq == 1:
            r_down.outward(dq)
            r_gate.across(dq)
            r_up.across(dq)
        parts = (n_dp if direct else 1) if final else None
        keep, give, *made = project_back(
            seq, scalars, x_window, dq, dk, dv, qkv_w, carry, parts, tokens_of(r_down, r_gate, r_up)
        )
        carry = made[0]
        if seq == 0:
            r_down.across(keep)
            r_gate.inward(keep)
            r_up.inward(keep)
        dx_half = keep.astype(f32) + sent(give, "tp", xor_perm(n_tp, 1)).astype(f32)
        total = dx_half[:, LONGEST : LONGEST + rows]
        at = LONGEST
        for far, take in steps:
            to_left = dx_half[:, at - take : at].astype(bf16)
            to_right = dx_half[:, window - at : window - at + take].astype(bf16)
            from_right = sent(to_left, "ctx", shift_perm(n_ctx, -far)).astype(f32)
            from_left = sent(to_right, "ctx", shift_perm(n_ctx, far)).astype(f32)
            pad = rows - take
            total = (
                total
                + jnp.pad(from_right, ((0, 0), (pad, 0), (0, 0)))
                + jnp.pad(from_left, ((0, 0), (0, pad), (0, 0)))
            )
            at -= take
        half_sums.append(total.astype(bf16))
    r_gate.outward(carry)
    r_up.outward(carry)
    if direct and n_ctx == 4 and own_rows % 64 == 0:
        g_qkv = reduce_last(made, sizes, mine, scalars)
    else:
        g_qkv = Reduction(made, sizes, mine, scalars, "last").first().second().inward().across().outward().result()
    half_in = jnp.concatenate(half_sums, 0)
    dinput = join_tp(half_in, sent(half_in, "tp", xor_perm(n_tp, 1)), me_tp).reshape(count, width)
    d_tokens = (dresid + dinput.astype(f32)).astype(bf16).reshape(seqs, rows, width)
    g_up = r_up.result()
    small = g_up[:, hidden + local : hidden + local + 4].T
    return (
        output,
        d_tokens,
        g_qkv.reshape(own_rows, 3, local),
        g_up[:, hidden : hidden + local],
        r_gate.result(),
        g_up[:, :hidden],
        r_down.result(),
        small[0],
        small[1],
        small[2],
        small[3],
    )


def solution(mesh):
    sizes = (mesh.shape["dp"], mesh.shape["ctx"], mesh.shape["tp"])
    wide, flat, kinds, square, line = (
        P("dp", "ctx", None),
        P("dp", "ctx"),
        P("dp", None, "tp"),
        P("dp", "tp"),
        P("dp"),
    )
    return jax.shard_map(
        functools.partial(body, sizes),
        mesh=mesh,
        in_specs=(wide, flat, wide, kinds) + (square,) * 4 + (line,) * 4,
        out_specs=(wide, wide, kinds) + (square,) * 4 + (line,) * 4,
        check_vma=False,
    )
```
